256 devices in a mesh: site: 8 (over y, core), row: 32 (over z, x).
Axes of the slice: x: 4, y: 4, z: 8, core: 2. Of those that a mesh axis runs over, the one named last changes fastest.
Arguments:
- mps_cores: bfloat16 [8, 64, 4, 128, 128], P('site', None, None, 'row'), may hold values from -1 to 1
- live_sizes: int32 [8, 64], P('site', 'row'), may hold values from 32 to 128, as said below
- retained_sizes: int32 [8, 64], P('site', 'row'), may hold values from 32 to 128, as said below
- pattern: int32 [8, 64, 4], P('site', 'row'), may hold values from 0 to 1, as said below
Outputs:
- ortho_cores: float32 [8, 64, 4, 128, 128], P('site', None, None, 'row')
- bond_factor: float32 [8, 64, 128, 128], P('site', None, 'row')
The draws below stay inside these ranges and needn't reach their ends.
Inputs may be any that keep to these rules, and one draw needn't show every extreme that they name: live_sizes[0, 0] = 128; for every core k and sector s, retained_sizes[k, s] <= live_sizes[k, s], and live_sizes[k + 1, s] <= retained_sizes[k, s]. retained_sizes[0, 0] = 128. pattern[k, s, 0] = 1 for every core k and sector s.
All inputs are finite; a program needn't handle non-finite values.
Results may differ from the reference program's by a relative error of at most 0.0003.
Values may be sent and summed in bfloat16 or wider, within the bound.
No kernel may reach another device: no remote copies, remote signals or barrier semaphores. Data moves between devices by JAX's collectives and lax.ppermute only.
A program may use at most 64 MiB of HBM per device.

```python
import math
import jax
import jax.numpy as jnp
from jax import lax

SB = 128
PHYS = 4
NSEC = 64
CORES = 8


def draw_mps_cores(key, part):
    key_noise, key_gain = jax.random.split(jax.random.fold_in(key, 11))
    full_shape = (CORES, NSEC, PHYS, SB, SB)
    noise_part = 0.3 * jax.random.normal(key_noise, full_shape, jnp.float32)
    diag_gain = jnp.exp(jax.random.uniform(key_gain, (CORES, NSEC, PHYS, SB), jnp.float32, -0.2, 0.3))
    identity = jnp.eye(SB, dtype=jnp.float32)
    values = 0.45 * (diag_gain[..., None] * identity + noise_part / jnp.sqrt(jnp.float32(SB)))
    return values.astype(jnp.bfloat16)


def sector_sizes(key):
    key_first, key_cut, key_fall = jax.random.split(jax.random.fold_in(key, 23), 3)
    initial_sizes = SB - jax.random.randint(key_first, (NSEC,), 0, SB // 8 + 1, dtype=jnp.int32)
    initial_sizes = initial_sizes.at[0].set(SB)
    cut_down = jax.random.randint(key_cut, (CORES, NSEC), 0, SB // 32 + 1, dtype=jnp.int32)
    cut_down = cut_down.at[0, 0].set(0)
    fall_off = jax.random.randint(key_fall, (CORES, NSEC), 0, SB // 64 + 1, dtype=jnp.int32)
    active_sector_list = []
    kept_list = []
    current = initial_sizes
    for core_at in range(CORES):
        kept_now = current - cut_down[core_at]
        active_sector_list.append(current)
        kept_list.append(kept_now)
        current = kept_now - fall_off[core_at]
    return (jnp.stack(active_sector_list).astype(jnp.int32), jnp.stack(kept_list).astype(jnp.int32))


def draw_live_sizes(key, part):
    return sector_sizes(key)[0]


def draw_retained_sizes(key, part):
    return sector_sizes(key)[1]


def draw_pattern(key, part):
    random_bits = jax.random.randint(jax.random.fold_in(key, 37), (CORES, NSEC, PHYS), 0, 4, dtype=jnp.int32)
    present = jnp.minimum(random_bits, 1)
    first_state = (lax.broadcasted_iota(jnp.int32, (CORES, NSEC, PHYS), 2) == 0).astype(jnp.int32)
    return jnp.maximum(present, first_state)


def setup_inputs(seed: int = 0) -> dict:
    seeds = jax.random.split(jax.random.key(seed), 5)
    mps_cores = draw_mps_cores(jax.random.fold_in(seeds[4], 71), 0)
    live_sizes = draw_live_sizes(jax.random.fold_in(seeds[4], 71), 0)
    retained_sizes = draw_retained_sizes(jax.random.fold_in(seeds[4], 71), 0)
    pattern = draw_pattern(jax.random.fold_in(seeds[4], 71), 0)
    return {"mps_cores": mps_cores, "live_sizes": live_sizes, "retained_sizes": retained_sizes, "pattern": pattern}


CHARGE_SECTORS = (0, 1, 1, 2)

def sector_sources(previous, pattern_now):
    pieces = []
    for charge in CHARGE_SECTORS:
        moved = jnp.concatenate([jnp.zeros((charge,) + previous.shape[1:], jnp.float32), previous[:previous.shape[0] - charge]], axis=0)
        pieces.append(moved)
    return jnp.stack(pieces, axis=1) * pattern_now[:, :, None, None].astype(jnp.float32)

def factorize(sources, sector_block, active_current, kept_now):
    sectors = sector_block.shape[0]
    capacity = sector_block.shape[-1]
    absorbed = jnp.einsum('spxa,spab->sbpx', sources, sector_block.astype(jnp.float32), precision=lax.Precision.HIGHEST)
    positions = lax.broadcasted_iota(jnp.int32, (sectors, capacity), 1)
    live_mask = (positions < active_current.astype(jnp.int32)[:, None]).astype(jnp.float32)
    keep_mask = (positions < kept_now.astype(jnp.int32)[:, None]).astype(jnp.float32)
    stacked_rows = (absorbed * live_mask[:, :, None, None]).reshape(sectors, capacity, -1)
    gram_product = jnp.einsum('wik,wnk->win', stacked_rows, stacked_rows, precision=lax.Precision.HIGHEST)
    gram_product = gram_product + (1.0 - live_mask)[:, :, None] * jnp.eye(capacity, dtype=jnp.float32)
    tri_lower = jnp.linalg.cholesky(gram_product)
    factor = jnp.swapaxes(tri_lower, 1, 2) * keep_mask[:, :, None]
    return (tri_lower, stacked_rows, keep_mask, factor)

def finish(tri_lower, stacked_rows, keep_mask, scaling):
    quotient = jax.scipy.linalg.solve_triangular(tri_lower, stacked_rows, lower=True)
    quotient = quotient * keep_mask[:, :, None] * scaling
    sectors, capacity = keep_mask.shape
    return jnp.transpose(quotient.reshape(sectors, capacity, -1, capacity), (0, 2, 3, 1))

def reference(mps_cores, live_sizes, retained_sizes, pattern):
    scaling = math.sqrt(PHYS * SB)
    previous = jnp.broadcast_to(jnp.eye(SB, dtype=jnp.float32), (NSEC, SB, SB))
    ortho_list = []
    factor_list = []
    for core_at in range(CORES):
        sources = sector_sources(previous, pattern[core_at])
        tri_lower, stacked_rows, keep_mask, factor = factorize(sources, mps_cores[core_at], live_sizes[core_at], retained_sizes[core_at])
        ortho_list.append(finish(tri_lower, stacked_rows, keep_mask, scaling))
        factor_list.append(factor)
        previous = factor
    return (jnp.stack(ortho_list), jnp.stack(factor_list))
```

```python
import functools
import math

import jax
import jax.numpy as jnp
from jax import lax
from jax.experimental import pallas as pl
from jax.experimental.pallas import tpu as pltpu
from jax.sharding import PartitionSpec as P

SB = 128
PANEL = 8
BLOCKS = SB // PANEL
F32 = jnp.float32
BF16 = jnp.bfloat16
NN = (((1,), (0,)), ((), ()))
NT = (((1,), (1,)), ((), ()))
VMEM_SPEC = pl.BlockSpec(memory_space=pltpu.VMEM)
SMEM_SPEC = pl.BlockSpec(memory_space=pltpu.SMEM)


def dot(a, b, dims):
    return lax.dot_general(a, b, dims, preferred_element_type=F32)


def split(x, parts):
    out = []
    for _ in range(parts):
        piece = x.astype(BF16)
        out.append(piece)
        x = x - piece.astype(F32)
    return out


def lanes(shape=(PANEL, SB)):
    return lax.broadcasted_iota(jnp.int32, shape, 1)


def rows_of(shape=(PANEL, SB)):
    return lax.broadcasted_iota(jnp.int32, shape, 0)


def row_spread(x, i):
    return jnp.broadcast_to(x[i : i + 1, :], (PANEL, SB))


def lane_spread(x, j):
    index = jnp.full((PANEL, SB), j, jnp.int32)
    return jnp.take_along_axis(x, index, axis=1, mode="promise_in_bounds")


def eliminate(mats, inverse, emit):
    lane, sub = lanes(), rows_of()
    mats = [list(m) for m in mats]
    count = range(len(mats))
    es = [[jnp.where(lane == sub + PANEL * t, 1.0, 0.0) for t in range(BLOCKS)] for _ in count] if inverse else None
    for t in range(BLOCKS):
        base = PANEL * t
        head = [a[t] for a in mats]
        cols = [[lane_spread(head[q], base + i) for i in range(PANEL)] for q in count]
        nxt = t + 1 if t + 1 < BLOCKS else None
        far = range(t + 2, BLOCKS)
        near = [[lane_spread(mats[q][nxt], base + i) for i in range(PANEL)] if nxt else None for q in count]
        fc = [{u: [lane_spread(mats[q][u], base + i) for i in range(PANEL)] for u in far} for q in count]
        diag = [None for _ in count]
        ws = [[] for _ in count]
        wes = [[] for _ in count]
        ls = [{} for _ in count]
        for i in range(PANEL):
            for q in count:
                a = mats[q]
                c = cols[q][i]
                diag[q] = c if i == 0 else jnp.where(sub == i, c, diag[q])
                inv = row_spread(1.0 / c, i)
                li = jnp.where(sub > i, c, 0.0) * inv
                w = jnp.where(lane > base + i, row_spread(head[q], i), 0.0)
                wi = w * inv
                ws[q].append(wi)
                for m in range(i + 1, PANEL):
                    cols[q][m] = cols[q][m] - li * row_spread(cols[q][m], i)
                    ls[q][m, i] = row_spread(li, m)
                if i < PANEL - 1:
                    head[q] = head[q] - li * w
                if inverse:
                    e = es[q]
                    erow = row_spread(e[t], i)
                    we = erow * inv
                    wes[q].append(we)
                    if i < PANEL - 1:
                        e[t] = e[t] - li * erow
                if nxt:
                    ci = near[q][i]
                    a[nxt] = a[nxt] - ci * wi
                    if inverse:
                        e[nxt] = e[nxt] - ci * we
                    for m in range(i + 1, PANEL):
                        near[q][m] = near[q][m] - ci * ls[q][m, i]
        for q in count:
            emit(q, t, head[q], diag[q], es[q][t] if inverse else None)
        if not len(far):
            continue
        for q in count:
            targets = [(ws[q], mats[q])] + ([(wes[q], es[q])] if inverse else [])
            for z, dest in targets:
                for i in range(PANEL - 2, -1, -1):
                    for m in range(PANEL - 1, i, -1):
                        z[i] = z[i] - ls[q][m, i] * z[m]
                for u in far:
                    total = fc[q][u][0] * z[0]
                    for i in range(1, PANEL):
                        total = total + fc[q][u][i] * z[i]
                    dest[u] = dest[u] - total


ORDER = ((0, 0), (1, 1), (1, 2), (1, 0), (0, 1), (0, 2), (1, 3), (0, 3))
GROUPS = (((0, 0), 0, 3), ((0, 1), 3, 1), ((1, 1), 4, 3), ((1, 0), 7, 1))


def factors(flags, own_refs, low_refs):
    shape = (SB, SB)
    eye = rows_of(shape) == lanes(shape)
    first = flags[1] == 1
    own_eye = jnp.where(eye, 1.0, 0.0)
    low_eye = jnp.where(eye & (flags[2] == 1), 1.0, 0.0)
    out = {}
    for which in range(2):
        own = own_refs[0][which]
        for more in own_refs[1:]:
            own = own + more[which]
        low = low_refs[0][which]
        for more in low_refs[1:]:
            low = low + more[which]
        out[0, which] = jnp.where(first, own_eye, own)
        out[1, which] = jnp.where(first, low_eye, low)
    return out


def grams(flags, parts_of, at_ref):
    blocks = {}
    for key, start, number in GROUPS:
        lhs = at_ref[start * SB : (start + number) * SB, :]
        total = None
        for piece in reversed(parts_of[key]):
            term = dot(lhs, piece, NT)
            total = term if total is None else total + term
        for k in range(number):
            blocks[ORDER[start + k]] = total[k * SB : (k + 1) * SB, :]
    mats = []
    lane, sub = lanes(), rows_of()
    for s in range(2):
        stacked = jnp.concatenate([blocks[s, p] for p in range(4)], axis=1)
        b1, b2, b3 = split(stacked, 3)
        gram = dot(b2, b2, NT) + (dot(b1, b3, NT) + dot(b3, b1, NT))
        gram = gram + (dot(b1, b2, NT) + dot(b2, b1, NT))
        gram = gram + dot(b1, b1, NT)
        live = flags[3 + s]
        slabs = []
        for t in range(BLOCKS):
            row = sub + PANEL * t
            dead = (row == lane) & (row >= live)
            slabs.append(gram[PANEL * t : PANEL * (t + 1), :] + jnp.where(dead, 1.0, 0.0))
        mats.append(slabs)
    return mats


def round_kernel(flags, own_ref, low_ref, at_ref, out_ref):
    @pl.when(flags[0] == 1)
    def _():
        found = factors(flags, [own_ref], [low_ref])
        mats = grams(flags, {k: split(v, 3) for k, v in found.items()}, at_ref)
        lane, sub = lanes(), rows_of()

        def emit(q, t, head, diag, _):
            row = sub + PANEL * t
            keep = (lane >= row) & (row < flags[5 + q])
            out_ref[q, PANEL * t : PANEL * (t + 1), :] = jnp.where(keep, head * lax.rsqrt(diag), 0.0)

        eliminate(mats, False, emit)


def last_kernel(flags, own_a, own_b, low_a, low_b, at_ref, a_ref, out_ref, w_ref, u_ref):
    found = factors(flags, [own_a, own_b], [low_a, low_b])
    mats = grams(flags, {k: split(v, 3) for k, v in found.items()}, at_ref)
    lane, sub = lanes(), rows_of()
    scaling = math.sqrt(4 * SB)

    def emit(q, t, head, diag, inv_rows):
        row = sub + PANEL * t
        kept = row < flags[5 + q]
        root = lax.rsqrt(diag)
        u_ref[q, PANEL * t : PANEL * (t + 1), :] = jnp.where((lane >= row) & kept, head * root, 0.0)
        w_ref[q, PANEL * t : PANEL * (t + 1), :] = jnp.where(kept, inv_rows * (root * scaling), 0.0)

    eliminate(mats, True, emit)
    pair = {k: split(v, 2) for k, v in found.items()}
    met = {}
    for key, start, number in GROUPS:
        for k in range(number):
            met[ORDER[start + k]] = (key, start + k)
    for s in range(2):
        w_hi, w_lo = split(w_ref[s], 2)
        for p in range(4):
            key, at = met[s, p]
            core = a_ref[at * SB : (at + 1) * SB, :]
            turned = dot(core, w_lo, NT) + dot(core, w_hi, NT)
            t_hi, t_lo = split(turned, 2)
            p_hi, p_lo = pair[key]
            block = (dot(p_lo, t_hi, NN) + dot(p_hi, t_lo, NN)) + dot(p_hi, t_hi, NN)
            out_ref[:, s * 16 + p * 4 : s * 16 + p * 4 + 4, :] = block.reshape(32, 4, SB)
        out_ref[:, 32 + 4 * s : 36 + 4 * s, :] = u_ref[s].reshape(32, 4, SB)


def shards(mps_cores, live_sizes, retained_sizes, pattern):
    n_site = lax.axis_size("site")
    n_row = lax.axis_size("row")
    site_at = lax.axis_index("site")
    row_at = lax.axis_index("row")
    sent = mps_cores.reshape(n_row, 32, SB)
    got = lax.all_to_all(sent, "row", split_axis=0, concat_axis=0, tiled=True)
    got = got.reshape(n_row, 2, 4, 4, SB)
    live, kept = live_sizes[0], retained_sizes[0]
    column = lax.broadcasted_iota(jnp.int32, (2, 4, SB), 2)
    mask = (column < live[:, None, None]) & (pattern[0][:, :, None] != 0)
    cores = jnp.transpose(got, (1, 2, 0, 3, 4)).reshape(2, 4, SB, SB)
    cores = jnp.where(mask[:, :, None, :], cores, jnp.zeros((), cores.dtype))
    stacked = jnp.stack([cores[s, p] for s, p in ORDER])
    a_all = stacked.reshape(8 * SB, SB)
    at_all = jnp.swapaxes(stacked, 1, 2).reshape(8 * SB, SB)
    site_first = (site_at == 0).astype(jnp.int32)
    has_lower = (row_at > 0).astype(jnp.int32)

    def flags_of(run):
        head = jnp.stack([run.astype(jnp.int32), site_first, has_lower])
        return jnp.concatenate([head, live, kept])

    packet = jax.ShapeDtypeStruct((2, SB, SB), F32)
    one_round = pl.pallas_call(
        round_kernel,
        out_shape=packet,
        in_specs=[SMEM_SPEC, VMEM_SPEC, VMEM_SPEC, VMEM_SPEC],
        out_specs=VMEM_SPEC,
        name="round",
    )
    own = low = jnp.zeros((2, SB, SB), F32)
    own_sum, low_sum = own, low
    for at in range(n_site - 1):
        factor = one_round(flags_of(site_at == at), own, low, at_all)
        here, there = n_row * at, n_row * (at + 1)
        own_next = lax.ppermute(factor, ("site", "row"), [(here + i, there + i) for i in range(n_row)])
        low_next = lax.ppermute(factor, ("site", "row"), [(here + i, there + i + 1) for i in range(n_row - 1)])
        if at:
            own_sum, low_sum = own_sum + own, low_sum + low
        own, low = own_next, low_next
    out = pl.pallas_call(
        last_kernel,
        out_shape=jax.ShapeDtypeStruct((32, 40, SB), F32),
        in_specs=[SMEM_SPEC] + [VMEM_SPEC] * 6,
        out_specs=VMEM_SPEC,
        scratch_shapes=[pltpu.VMEM((2, SB, SB), F32), pltpu.VMEM((2, SB, SB), F32)],
        name="last",
    )(flags_of(site_at == 0), own_sum, own, low_sum, low, at_all, a_all)
    back = lax.all_to_all(out, "row", split_axis=0, concat_axis=0, tiled=True)
    ortho = back[:, :32].reshape(1, 2 * n_row, 4, 4, SB)
    factor = back[:, 32:].reshape(1, 2 * n_row, 4, SB)
    return (ortho, factor)


def solution(mesh):
    in_specs = (
        P("site", None, None, "row", None),
        P("site", "row"),
        P("site", "row"),
        P("site", "row", None),
    )
    out_specs = (P("site", None, None, "row", None), P("site", None, "row", None))
    return jax.shard_map(shards, mesh=mesh, in_specs=in_specs, out_specs=out_specs, check_vma=False)
```

```python
import functools
import math

import jax
import jax.numpy as jnp
from jax import lax
from jax.experimental import pallas as pl
from jax.experimental.pallas import tpu as pltpu
from jax.sharding import PartitionSpec as P

SB = 128
PANEL = 8
F32 = jnp.float32
BF16 = jnp.bfloat16
NN = (((1,), (0,)), ((), ()))
NT = (((1,), (1,)), ((), ()))
TN = (((0,), (0,)), ((), ()))
VMEM_BYTES = 24 * 1024 * 1024
VMEM_SPEC = pl.BlockSpec(memory_space=pltpu.VMEM)
SMEM_SPEC = pl.BlockSpec(memory_space=pltpu.SMEM)


def dot(a, b, dims):
    return lax.dot_general(a, b, dims, preferred_element_type=F32)


def split(x, parts):
    out = []
    for _ in range(parts):
        piece = x.astype(BF16)
        out.append(piece)
        x = x - piece.astype(F32)
    return out


HALF = SB // 2
SLABS = HALF // PANEL


def lanes(shape=(PANEL, SB)):
    return lax.broadcasted_iota(jnp.int32, shape, 1)


def rows_of(shape=(PANEL, SB)):
    return lax.broadcasted_iota(jnp.int32, shape, 0)


def row_spread(x, i):
    return jnp.broadcast_to(x[i : i + 1, :], (PANEL, SB))


def sweep(main, others, emit):
    lane, sub = lanes(), rows_of()
    high = jnp.where(lane >= HALF, HALF, 0)

    def spread(x, j):
        return jnp.take_along_axis(x, high + j, axis=1, mode="promise_in_bounds")

    tables = [list(main)] + [list(o) for o in others]
    for t in range(SLABS):
        base = PANEL * t
        cols = [spread(tables[0][t], base + i) for i in range(PANEL)]
        nxt = t + 1 if t + 1 < SLABS else None
        far = range(t + 2, SLABS)
        near = [spread(tables[0][nxt], base + i) for i in range(PANEL)] if nxt else None
        fc = {u: [spread(tables[0][u], base + i) for i in range(PANEL)] for u in far}
        diag = None
        ws = [[] for _ in tables]
        ls = {}
        for i in range(PANEL):
            c = cols[i]
            diag = c if i == 0 else jnp.where(sub == i, c, diag)
            inv = row_spread(1.0 / c, i)
            li = jnp.where(sub > i, c, 0.0) * inv
            for m in range(i + 1, PANEL):
                cols[m] = cols[m] - li * row_spread(cols[m], i)
                ls[m, i] = row_spread(li, m)
            for w, table in zip(ws, tables):
                row = row_spread(table[t], i)
                w.append(row * inv)
                if i < PANEL - 1:
                    table[t] = table[t] - li * row
                if nxt:
                    table[nxt] = table[nxt] - near[i] * w[i]
            if nxt:
                for m in range(i + 1, PANEL):
                    near[m] = near[m] - near[i] * ls[m, i]
        emit(t, tables[0][t], [table[t] for table in tables[1:]], diag)
        if not len(far):
            continue
        for z, table in zip(ws, tables):
            for i in range(PANEL - 2, -1, -1):
                for m in range(PANEL - 1, i, -1):
                    z[i] = z[i] - ls[m, i] * z[m]
            for u in far:
                total = fc[u][0] * z[0]
                for i in range(1, PANEL):
                    total = total + fc[u][i] * z[i]
                table[u] = table[u] - total


ORDER = ((0, 0), (1, 1), (1, 2), (1, 0), (0, 1), (0, 2), (1, 3), (0, 3))
GROUPS = (((0, 0), 0, 3), ((0, 1), 3, 1), ((1, 1), 4, 3), ((1, 0), 7, 1))
PACKET = (3 * HALF, SB)


def assembled(packet):
    left = lanes((HALF, SB)) < HALF
    u11, u12, u22 = (packet[HALF * k : HALF * (k + 1), :] for k in range(3))
    r11, r12, r22 = (pltpu.roll(u, HALF, 1) for u in (u11, u12, u22))
    first = jnp.concatenate([jnp.where(left, u11, r12), jnp.where(left, 0.0, r22)], axis=0)
    second = jnp.concatenate([jnp.where(left, r11, u12), jnp.where(left, 0.0, u22)], axis=0)
    return first, second


def factors(flags, own, low):
    shape = (SB, SB)
    eye = rows_of(shape) == lanes(shape)
    first = flags[1] == 1
    own_eye = jnp.where(eye, 1.0, 0.0)
    low_eye = jnp.where(eye & (flags[2] == 1), 1.0, 0.0)
    out = {}
    for which, value in enumerate(assembled(own)):
        out[0, which] = jnp.where(first, own_eye, value)
    for which, value in enumerate(assembled(low)):
        out[1, which] = jnp.where(first, low_eye, value)
    return out


def product(a, b, dims):
    total = dot(a[1], b[1], dims) + (dot(a[0], b[2], dims) + dot(a[2], b[0], dims))
    total = total + (dot(a[0], b[1], dims) + dot(a[1], b[0], dims))
    return total + dot(a[0], b[0], dims)


def halves(both):
    return jnp.where(lanes((HALF, SB)) < HALF, both[:HALF, :], both[HALF:, :])


def slabs_of(x):
    return [x[PANEL * t : PANEL * (t + 1), :] for t in range(SLABS)]


def grams(flags, parts_of, at_ref):
    blocks = {}
    for key, start, number in GROUPS:
        lhs = at_ref[start * SB : (start + number) * SB, :]
        total = None
        for piece in reversed(parts_of[key]):
            term = dot(lhs, piece, NT)
            total = term if total is None else total + term
        for k in range(number):
            blocks[ORDER[start + k]] = total[k * SB : (k + 1) * SB, :]
    tops = jnp.concatenate([jnp.concatenate([blocks[s, p][:HALF, :] for s in range(2)], axis=0) for p in range(4)], axis=1)
    lows = jnp.concatenate([jnp.concatenate([blocks[s, p][HALF:, :] for s in range(2)], axis=0) for p in range(4)], axis=1)
    tops, lows = split(tops, 3), split(lows, 3)
    both = [jnp.concatenate([a, b], axis=0) for a, b in zip(tops, lows)]
    upper = product(tops, both, NT)
    shape = (HALF, SB)
    live = jnp.where(lanes(shape) < HALF, flags[3], flags[4])
    row = rows_of(shape)
    same = row == (lanes(shape) & (HALF - 1))
    g11 = halves(upper[:, :SB]) + jnp.where(same & (row >= live), 1.0, 0.0)
    g22 = halves(product(lows, lows, NT)) + jnp.where(same & (row + HALF >= live), 1.0, 0.0)
    return g11, halves(upper[:, SB:]), g22


def factorize(flags, parts_of, at_ref, u_ref, w_ref):
    g11, g12, g22 = grams(flags, parts_of, at_ref)
    lane, sub = lanes(), rows_of()
    place = lane & (HALF - 1)
    kept = jnp.where(lane < HALF, flags[5], flags[6])
    scaling = math.sqrt(4 * SB)
    eye = [jnp.where(place == sub + PANEL * t, 1.0, 0.0) for t in range(SLABS)]
    u12, w11 = [], []

    def first(t, head, rest, diag):
        row = sub + PANEL * t
        root = lax.rsqrt(diag)
        at = slice(PANEL * t, PANEL * (t + 1))
        u12.append(rest[0] * root)
        u_ref[at, :] = jnp.where((place >= row) & (row < kept), head * root, 0.0)
        u_ref[slice(at.start + HALF, at.stop + HALF), :] = jnp.where(row < kept, u12[t], 0.0)
        if w_ref is not None:
            w11.append(rest[1] * root)
            w_ref[at, :] = jnp.where(row < kept, w11[t] * scaling, 0.0)

    sweep(slabs_of(g11), [slabs_of(g12)] + ([eye] if w_ref is not None else []), first)
    cross = split(jnp.concatenate(u12, axis=0), 3)
    others = []
    if w_ref is not None:
        below = halves(product(cross, split(jnp.concatenate(w11, axis=0), 3), TN))
        others = [slabs_of(-below), eye]

    def second(t, head, rest, diag):
        row = sub + PANEL * t
        stay = row + HALF < kept
        root = lax.rsqrt(diag)
        u_ref[2 * HALF + PANEL * t : 2 * HALF + PANEL * (t + 1), :] = jnp.where((place >= row) & stay, head * root, 0.0)
        for k, value in enumerate(rest):
            at = HALF * (k + 1) + PANEL * t
            w_ref[at : at + PANEL, :] = jnp.where(stay, value * (root * scaling), 0.0)

    sweep(slabs_of(g22 - halves(product(cross, cross, TN))), others, second)


def round_kernel(at, flags, own_ref, low_ref, at_ref, _, out_ref, state_ref):
    @pl.when(flags[0] == at)
    def _():
        own, low = own_ref[...], low_ref[...]
        state_ref[0], state_ref[1] = own, low
        found = factors(flags, own, low)
        factorize(flags, {k: split(v, 3) for k, v in found.items()}, at_ref, out_ref, None)


def last_kernel(at, flags, own_ref, low_ref, state_ref, at_ref, a_ref, out_ref, w_ref, u_ref):
    here = flags[0] == at
    own = jnp.where(here, own_ref[...], state_ref[0])
    low = jnp.where(here, low_ref[...], state_ref[1])
    found = factors(flags, own, low)
    factorize(flags, {k: split(v, 3) for k, v in found.items()}, at_ref, u_ref, w_ref)
    pair = {k: split(v, 2) for k, v in found.items()}
    met = {}
    for key, start, number in GROUPS:
        for k in range(number):
            met[ORDER[start + k]] = (key, start + k)
    left = lanes((HALF, SB)) < HALF
    w11, w21, w22 = (w_ref[HALF * k : HALF * (k + 1), :] for k in range(3))
    r11, r21, r22 = (pltpu.roll(w, HALF, 1) for w in (w11, w21, w22))
    inverse = (
        jnp.concatenate([jnp.where(left, w11, 0.0), jnp.where(left, w21, r22)], axis=0),
        jnp.concatenate([jnp.where(left, r11, 0.0), jnp.where(left, r21, w22)], axis=0),
    )
    factor = assembled(u_ref[...])
    for s in range(2):
        w_hi, w_lo = split(inverse[s], 2)
        for p in range(4):
            key, start = met[s, p]
            core = a_ref[start * SB : (start + 1) * SB, :]
            turned = dot(core, w_lo, NT) + dot(core, w_hi, NT)
            t_hi, t_lo = split(turned, 2)
            p_hi, p_lo = pair[key]
            block = (dot(p_lo, t_hi, NN) + dot(p_hi, t_lo, NN)) + dot(p_hi, t_hi, NN)
            out_ref[:, s * 16 + p * 4 : s * 16 + p * 4 + 4, :] = block.reshape(32, 4, SB)
        out_ref[:, 32 + 4 * s : 36 + 4 * s, :] = factor[s].reshape(32, 4, SB)


def shards(mps_cores, live_sizes, retained_sizes, pattern):
    n_site = lax.axis_size("site")
    n_row = lax.axis_size("row")
    site_at = lax.axis_index("site")
    row_at = lax.axis_index("row")
    sent = mps_cores.reshape(n_row, 32, SB)
    got = lax.all_to_all(sent, "row", split_axis=0, concat_axis=0, tiled=True)
    got = got.reshape(n_row, 2, 4, 4, SB)
    live, kept = live_sizes[0], retained_sizes[0]
    column = lax.broadcasted_iota(jnp.int32, (2, 4, SB), 2)
    mask = (column < live[:, None, None]) & (pattern[0][:, :, None] != 0)
    cores = jnp.transpose(got, (1, 2, 0, 3, 4)).reshape(2, 4, SB, SB)
    cores = jnp.where(mask[:, :, None, :], cores, jnp.zeros((), cores.dtype))
    stacked = jnp.stack([cores[s, p] for s, p in ORDER])
    a_all = stacked.reshape(8 * SB, SB)
    at_all = jnp.swapaxes(stacked, 1, 2).reshape(8 * SB, SB)
    head = jnp.stack([site_at, (site_at == 0).astype(jnp.int32), (row_at > 0).astype(jnp.int32)])
    flags = jnp.concatenate([head.astype(jnp.int32), live, kept])
    params = pltpu.CompilerParams(vmem_limit_bytes=VMEM_BYTES)
    packet = jax.ShapeDtypeStruct(PACKET, F32)
    own = low = jnp.zeros(PACKET, F32)
    state = jnp.zeros((2,) + PACKET, F32)
    for at in range(n_site - 1):
        factor, state = pl.pallas_call(
            functools.partial(round_kernel, at),
            out_shape=(packet, jax.ShapeDtypeStruct(state.shape, F32)),
            in_specs=[SMEM_SPEC] + [VMEM_SPEC] * 4,
            out_specs=(VMEM_SPEC, VMEM_SPEC),
            input_output_aliases={4: 1},
            compiler_params=params,
            name="round",
        )(flags, own, low, at_all, state)
        here, there = n_row * at, n_row * (at + 1)
        low = lax.ppermute(factor, ("site", "row"), [(here + i, there + i + 1) for i in range(n_row - 1)])
        own = lax.ppermute(factor, ("site", "row"), [(here + i, there + i) for i in range(n_row)])
    out = pl.pallas_call(
        functools.partial(last_kernel, n_site - 1),
        out_shape=jax.ShapeDtypeStruct((32, 40, SB), F32),
        in_specs=[SMEM_SPEC] + [VMEM_SPEC] * 5,
        out_specs=VMEM_SPEC,
        scratch_shapes=[pltpu.VMEM(PACKET, F32), pltpu.VMEM(PACKET, F32)],
        compiler_params=params,
        name="last",
    )(flags, own, low, state, at_all, a_all)
    back = lax.all_to_all(out, "row", split_axis=0, concat_axis=0, tiled=True)
    ortho = back[:, :32].reshape(1, 2 * n_row, 4, 4, SB)
    factor = back[:, 32:].reshape(1, 2 * n_row, 4, SB)
    return (ortho, factor)


def solution(mesh):
    in_specs = (
        P("site", None, None, "row", None),
        P("site", "row"),
        P("site", "row"),
        P("site", "row", None),
    )
    out_specs = (P("site", None, None, "row", None), P("site", None, "row", None))
    return jax.shard_map(shards, mesh=mesh, in_specs=in_specs, out_specs=out_specs, check_vma=False)
```

```python
import functools
import math

import jax
import jax.numpy as jnp
from jax import lax
from jax.experimental import pallas as pl
from jax.experimental.pallas import tpu as pltpu
from jax.sharding import PartitionSpec as P

SB = 128
PANEL = 8
F32 = jnp.float32
BF16 = jnp.bfloat16
NN = (((1,), (0,)), ((), ()))
NT = (((1,), (1,)), ((), ()))
TN = (((0,), (0,)), ((), ()))
VMEM_BYTES = 24 * 1024 * 1024
VMEM_SPEC = pl.BlockSpec(memory_space=pltpu.VMEM)
SMEM_SPEC = pl.BlockSpec(memory_space=pltpu.SMEM)


def dot(a, b, dims):
    return lax.dot_general(a, b, dims, preferred_element_type=F32)


def split(x, parts):
    out = []
    for _ in range(parts):
        piece = x.astype(BF16)
        out.append(piece)
        x = x - piece.astype(F32)
    return out


HALF = SB // 2
SLABS = HALF // PANEL


def lanes(shape=(PANEL, SB)):
    return lax.broadcasted_iota(jnp.int32, shape, 1)


def rows_of(shape=(PANEL, SB)):
    return lax.broadcasted_iota(jnp.int32, shape, 0)


def row_spread(x, i):
    return jnp.broadcast_to(x[i : i + 1, :], (PANEL, SB))


def sweep(main, others, emit):
    lane, sub = lanes(), rows_of()
    high = jnp.where(lane >= HALF, HALF, 0)

    def spread(x, j):
        return jnp.take_along_axis(x, high + j, axis=1, mode="promise_in_bounds")

    tables = [list(main)] + [list(o) for o in others]
    for t in range(SLABS):
        base = PANEL * t
        cols = [spread(tables[0][t], i) for i in range(PANEL)] if t == 0 else ahead
        nxt = t + 1 if t + 1 < SLABS else None
        ahead = [spread(tables[0][nxt], base + PANEL + i) for i in range(PANEL)] if nxt else None
        close = range(t + 1, min(t + 2 + 1, SLABS))
        far = range(t + 2 + 1, SLABS)
        near = {u: [spread(tables[0][u], base + i) for i in range(PANEL)] for u in close}
        fc = {u: [spread(tables[0][u], base + i) for i in range(PANEL)] for u in far}
        diag = None
        ws = [[] for _ in tables]
        ls = {}
        for i in range(PANEL):
            c = cols[i]
            diag = c if i == 0 else jnp.where(sub == i, c, diag)
            inv = row_spread(1.0 / c, i)
            li = jnp.where(sub > i, c, 0.0) * inv
            for m in range(i + 1, PANEL):
                cols[m] = cols[m] - li * row_spread(cols[m], i)
                ls[m, i] = row_spread(li, m)
            for w, table in zip(ws, tables):
                row = row_spread(table[t], i)
                w.append(row * inv)
                if i < PANEL - 1:
                    table[t] = table[t] - li * row
                for u in close:
                    table[u] = table[u] - near[u][i] * w[i]
            for u in close:
                for m in range(i + 1, PANEL):
                    near[u][m] = near[u][m] - near[u][i] * ls[m, i]
            if nxt:
                part = near[nxt][i] * inv
                for m in range(PANEL):
                    ahead[m] = ahead[m] - near[nxt][i] * row_spread(part, m)
        emit(t, tables[0][t], [table[t] for table in tables[1:]], diag)
        if not len(far):
            continue
        for z, table in zip(ws, tables):
            for i in range(PANEL - 2, -1, -1):
                for m in range(PANEL - 1, i, -1):
                    z[i] = z[i] - ls[m, i] * z[m]
            for u in far:
                total = fc[u][0] * z[0]
                for i in range(1, PANEL):
                    total = total + fc[u][i] * z[i]
                table[u] = table[u] - total


ORDER = ((0, 0), (1, 1), (1, 2), (1, 0), (0, 1), (0, 2), (1, 3), (0, 3))
GROUPS = (((0, 0), 0, 3), ((0, 1), 3, 1), ((1, 1), 4, 3), ((1, 0), 7, 1))
PACKET = (3 * HALF, SB)


def assembled(packet):
    left = lanes((HALF, SB)) < HALF
    u11, u12, u22 = (packet[HALF * k : HALF * (k + 1), :] for k in range(3))
    r11, r12, r22 = (pltpu.roll(u, HALF, 1) for u in (u11, u12, u22))
    first = jnp.concatenate([jnp.where(left, u11, r12), jnp.where(left, 0.0, r22)], axis=0)
    second = jnp.concatenate([jnp.where(left, r11, u12), jnp.where(left, 0.0, u22)], axis=0)
    return first, second


def factors(flags, own, low):
    shape = (SB, SB)
    eye = rows_of(shape) == lanes(shape)
    first = flags[1] == 1
    own_eye = jnp.where(eye, 1.0, 0.0)
    low_eye = jnp.where(eye & (flags[2] == 1), 1.0, 0.0)
    out = {}
    for which, value in enumerate(assembled(own)):
        out[0, which] = jnp.where(first, own_eye, value)
    for which, value in enumerate(assembled(low)):
        out[1, which] = jnp.where(first, low_eye, value)
    return out


def product(a, b, dims):
    axes = dims[0][0][0], dims[0][1][0]
    left = jnp.concatenate([a[k] for k in (1, 0, 2, 0, 1, 0)], axis=axes[0])
    right = jnp.concatenate([b[k] for k in (1, 2, 0, 1, 0, 0)], axis=axes[1])
    return dot(left, right, dims)


def halves(both):
    return jnp.where(lanes((HALF, SB)) < HALF, both[:HALF, :], both[HALF:, :])


def slabs_of(x):
    return [x[PANEL * t : PANEL * (t + 1), :] for t in range(SLABS)]


def grams(flags, parts_of, at_ref):
    blocks = {}
    for key, start, number in GROUPS:
        lhs = at_ref[start * SB : (start + number) * SB, :]
        pieces = parts_of[key]
        total = dot(jnp.concatenate([lhs] * len(pieces), axis=1), jnp.concatenate(pieces[::-1], axis=1), NT)
        for k in range(number):
            blocks[ORDER[start + k]] = total[k * SB : (k + 1) * SB, :]
    tops = jnp.concatenate([jnp.concatenate([blocks[s, p][:HALF, :] for s in range(2)], axis=0) for p in range(4)], axis=1)
    lows = jnp.concatenate([jnp.concatenate([blocks[s, p][HALF:, :] for s in range(2)], axis=0) for p in range(4)], axis=1)
    tops, lows = split(tops, 3), split(lows, 3)
    both = [jnp.concatenate([a, b], axis=0) for a, b in zip(tops, lows)]
    upper = product(tops, both, NT)
    shape = (HALF, SB)
    live = jnp.where(lanes(shape) < HALF, flags[3], flags[4])
    row = rows_of(shape)
    same = row == (lanes(shape) & (HALF - 1))
    g11 = halves(upper[:, :SB]) + jnp.where(same & (row >= live), 1.0, 0.0)
    g22 = halves(product(lows, lows, NT)) + jnp.where(same & (row + HALF >= live), 1.0, 0.0)
    return g11, halves(upper[:, SB:]), g22


def factorize(flags, parts_of, at_ref, u_ref, w_ref):
    g11, g12, g22 = grams(flags, parts_of, at_ref)
    lane, sub = lanes(), rows_of()
    place = lane & (HALF - 1)
    kept = jnp.where(lane < HALF, flags[5], flags[6])
    scaling = math.sqrt(4 * SB)
    eye = [jnp.where(place == sub + PANEL * t, 1.0, 0.0) for t in range(SLABS)]
    u12, w11 = [], []

    def first(t, head, rest, diag):
        row = sub + PANEL * t
        root = lax.rsqrt(diag)
        at = slice(PANEL * t, PANEL * (t + 1))
        u12.append(rest[0] * root)
        u_ref[at, :] = jnp.where((place >= row) & (row < kept), head * root, 0.0)
        u_ref[slice(at.start + HALF, at.stop + HALF), :] = jnp.where(row < kept, u12[t], 0.0)
        if w_ref is not None:
            w11.append(rest[1] * root)
            w_ref[at, :] = jnp.where(row < kept, w11[t] * scaling, 0.0)

    sweep(slabs_of(g11), [slabs_of(g12)] + ([eye] if w_ref is not None else []), first)
    cross = split(jnp.concatenate(u12, axis=0), 3)
    others = []
    if w_ref is not None:
        below = halves(product(cross, split(jnp.concatenate(w11, axis=0), 3), TN))
        others = [slabs_of(-below), eye]

    def second(t, head, rest, diag):
        row = sub + PANEL * t
        stay = row + HALF < kept
        root = lax.rsqrt(diag)
        u_ref[2 * HALF + PANEL * t : 2 * HALF + PANEL * (t + 1), :] = jnp.where((place >= row) & stay, head * root, 0.0)
        for k, value in enumerate(rest):
            at = HALF * (k + 1) + PANEL * t
            w_ref[at : at + PANEL, :] = jnp.where(stay, value * (root * scaling), 0.0)

    sweep(slabs_of(g22 - halves(product(cross, cross, TN))), others, second)


def round_kernel(at, flags, own_ref, low_ref, at_ref, _, out_ref, state_ref):
    @pl.when(flags[0] == at)
    def _():
        own, low = own_ref[...], low_ref[...]
        state_ref[0], state_ref[1] = own, low
        found = factors(flags, own, low)
        factorize(flags, {k: split(v, 3) for k, v in found.items()}, at_ref, out_ref, None)


def last_kernel(at, flags, own_ref, low_ref, state_ref, at_ref, a_ref, out_ref, w_ref, u_ref):
    here = flags[0] == at
    own = jnp.where(here, own_ref[...], state_ref[0])
    low = jnp.where(here, low_ref[...], state_ref[1])
    found = factors(flags, own, low)
    factorize(flags, {k: split(v, 3) for k, v in found.items()}, at_ref, u_ref, w_ref)
    pair = {k: split(v, 2) for k, v in found.items()}
    met = {}
    for key, start, number in GROUPS:
        for k in range(number):
            met[ORDER[start + k]] = (key, start + k)
    left = lanes((HALF, SB)) < HALF
    w11, w21, w22 = (w_ref[HALF * k : HALF * (k + 1), :] for k in range(3))
    r11, r21, r22 = (pltpu.roll(w, HALF, 1) for w in (w11, w21, w22))
    inverse = (
        jnp.concatenate([jnp.where(left, w11, 0.0), jnp.where(left, w21, r22)], axis=0),
        jnp.concatenate([jnp.where(left, r11, 0.0), jnp.where(left, r21, w22)], axis=0),
    )
    factor = assembled(u_ref[...])
    for s in range(2):
        w_hi, w_lo = split(inverse[s], 2)
        for p in range(4):
            key, start = met[s, p]
            core = a_ref[start * SB : (start + 1) * SB, :]
            turned = dot(core, w_lo, NT) + dot(core, w_hi, NT)
            t_hi, t_lo = split(turned, 2)
            p_hi, p_lo = pair[key]
            block = (dot(p_lo, t_hi, NN) + dot(p_hi, t_lo, NN)) + dot(p_hi, t_hi, NN)
            out_ref[:, s * 16 + p * 4 : s * 16 + p * 4 + 4, :] = block.reshape(32, 4, SB)
        out_ref[:, 32 + 4 * s : 36 + 4 * s, :] = factor[s].reshape(32, 4, SB)


def shards(mps_cores, live_sizes, retained_sizes, pattern):
    n_site = lax.axis_size("site")
    n_row = lax.axis_size("row")
    site_at = lax.axis_index("site")
    row_at = lax.axis_index("row")
    sent = mps_cores.reshape(n_row, 32, SB)
    got = lax.all_to_all(sent, "row", split_axis=0, concat_axis=0, tiled=True)
    got = got.reshape(n_row, 2, 4, 4, SB)
    live, kept = live_sizes[0], retained_sizes[0]
    column = lax.broadcasted_iota(jnp.int32, (2, 4, SB), 2)
    mask = (column < live[:, None, None]) & (pattern[0][:, :, None] != 0)
    cores = jnp.transpose(got, (1, 2, 0, 3, 4)).reshape(2, 4, SB, SB)
    cores = jnp.where(mask[:, :, None, :], cores, jnp.zeros((), cores.dtype))
    stacked = jnp.stack([cores[s, p] for s, p in ORDER])
    a_all = stacked.reshape(8 * SB, SB)
    at_all = jnp.swapaxes(stacked, 1, 2).reshape(8 * SB, SB)
    head = jnp.stack([site_at, (site_at == 0).astype(jnp.int32), (row_at > 0).astype(jnp.int32)])
    flags = jnp.concatenate([head.astype(jnp.int32), live, kept])
    params = pltpu.CompilerParams(vmem_limit_bytes=VMEM_BYTES)
    packet = jax.ShapeDtypeStruct(PACKET, F32)
    own = low = jnp.zeros(PACKET, F32)
    state = jnp.zeros((2,) + PACKET, F32)
    for at in range(n_site - 1):
        factor, state = pl.pallas_call(
            functools.partial(round_kernel, at),
            out_shape=(packet, jax.ShapeDtypeStruct(state.shape, F32)),
            in_specs=[SMEM_SPEC] + [VMEM_SPEC] * 4,
            out_specs=(VMEM_SPEC, VMEM_SPEC),
            input_output_aliases={4: 1},
            compiler_params=params,
            name="round",
        )(flags, own, low, at_all, state)
        here, there = n_row * at, n_row * (at + 1)
        low = lax.ppermute(factor, ("site", "row"), [(here + i, there + i + 1) for i in range(n_row - 1)])
        own = lax.ppermute(factor, ("site", "row"), [(here + i, there + i) for i in range(n_row)])
    out = pl.pallas_call(
        functools.partial(last_kernel, n_site - 1),
        out_shape=jax.ShapeDtypeStruct((32, 40, SB), F32),
        in_specs=[SMEM_SPEC] + [VMEM_SPEC] * 5,
        out_specs=VMEM_SPEC,
        scratch_shapes=[pltpu.VMEM(PACKET, F32), pltpu.VMEM(PACKET, F32)],
        compiler_params=params,
        name="last",
    )(flags, own, low, state, at_all, a_all)
    back = lax.all_to_all(out, "row", split_axis=0, concat_axis=0, tiled=True)
    ortho = back[:, :32].reshape(1, 2 * n_row, 4, 4, SB)
    factor = back[:, 32:].reshape(1, 2 * n_row, 4, SB)
    return (ortho, factor)


def solution(mesh):
    in_specs = (
        P("site", None, None, "row", None),
        P("site", "row"),
        P("site", "row"),
        P("site", "row", None),
    )
    out_specs = (P("site", None, None, "row", None), P("site", None, "row", None))
    return jax.shard_map(shards, mesh=mesh, in_specs=in_specs, out_specs=out_specs, check_vma=False)
```

```python
import functools
import math

import jax
import jax.numpy as jnp
from jax import lax
from jax.experimental import pallas as pl
from jax.experimental.pallas import tpu as pltpu
from jax.sharding import PartitionSpec as P

SB = 128
PANEL = 8
F32 = jnp.float32
BF16 = jnp.bfloat16
NN = (((1,), (0,)), ((), ()))
NT = (((1,), (1,)), ((), ()))
TN = (((0,), (0,)), ((), ()))
VMEM_BYTES = 24 * 1024 * 1024
VMEM_SPEC = pl.BlockSpec(memory_space=pltpu.VMEM)
SMEM_SPEC = pl.BlockSpec(memory_space=pltpu.SMEM)


def dot(a, b, dims):
    return lax.dot_general(a, b, dims, preferred_element_type=F32)


def split(x, parts):
    out = []
    for _ in range(parts):
        piece = x.astype(BF16)
        out.append(piece)
        x = x - piece.astype(F32)
    return out


HALF = SB // 2
SLABS = HALF // PANEL


def lanes(shape=(PANEL, SB)):
    return lax.broadcasted_iota(jnp.int32, shape, 1)


def rows_of(shape=(PANEL, SB)):
    return lax.broadcasted_iota(jnp.int32, shape, 0)


def row_spread(x, i):
    return jnp.broadcast_to(x[i : i + 1, :], (PANEL, SB))


def sweep(main, others, emit):
    lane, sub = lanes(), rows_of()
    high = jnp.where(lane >= HALF, HALF, 0)

    def spread(x, j):
        return jnp.take_along_axis(x, high + j, axis=1, mode="promise_in_bounds")

    tables = [list(main)] + [list(o) for o in others]
    for t in range(SLABS):
        base = PANEL * t
        cols = [spread(tables[0][t], i) for i in range(PANEL)] if t == 0 else ahead
        nxt = t + 1 if t + 1 < SLABS else None
        ahead = [spread(tables[0][nxt], base + PANEL + i) for i in range(PANEL)] if nxt else None
        close = range(t + 1, min(t + 2 + 1, SLABS))
        far = range(t + 2 + 1, SLABS)
        near = {u: [spread(tables[0][u], base + i) for i in range(PANEL)] for u in close}
        fc = {u: [spread(tables[0][u], base + i) for i in range(PANEL)] for u in far}
        diag = None
        ws = [[] for _ in tables]
        ls = {}
        for i in range(PANEL):
            c = cols[i]
            diag = c if i == 0 else jnp.where(sub == i, c, diag)
            inv = row_spread(1.0 / c, i)
            li = jnp.where(sub > i, c, 0.0) * inv
            for m in range(i + 1, PANEL):
                cols[m] = cols[m] - li * row_spread(cols[m], i)
                ls[m, i] = row_spread(li, m)
            for w, table in zip(ws, tables):
                row = row_spread(table[t], i)
                w.append(row * inv)
                if i < PANEL - 1:
                    table[t] = table[t] - li * row
                for u in close:
                    table[u] = table[u] - near[u][i] * w[i]
            for u in close:
                for m in range(i + 1, PANEL):
                    near[u][m] = near[u][m] - near[u][i] * ls[m, i]
            if nxt:
                part = near[nxt][i] * inv
                for m in range(PANEL):
                    ahead[m] = ahead[m] - near[nxt][i] * row_spread(part, m)
        emit(t, tables[0][t], [table[t] for table in tables[1:]], diag)
        if not len(far):
            continue
        for z, table in zip(ws, tables):
            for i in range(PANEL - 2, -1, -1):
                for m in range(PANEL - 1, i, -1):
                    z[i] = z[i] - ls[m, i] * z[m]
            for u in far:
                total = fc[u][0] * z[0]
                for i in range(1, PANEL):
                    total = total + fc[u][i] * z[i]
                table[u] = table[u] - total


ORDER = ((0, 0), (1, 1), (1, 2), (1, 0), (0, 1), (0, 2), (1, 3), (0, 3))
GROUPS = (((0, 0), 0, 3), ((0, 1), 3, 1), ((1, 1), 4, 3), ((1, 0), 7, 1))
PACKET = (3 * HALF, SB)


def assembled(packet):
    left = lanes((HALF, SB)) < HALF
    u11, u12, u22 = (packet[HALF * k : HALF * (k + 1), :] for k in range(3))
    r11, r12, r22 = (pltpu.roll(u, HALF, 1) for u in (u11, u12, u22))
    first = jnp.concatenate([jnp.where(left, u11, r12), jnp.where(left, 0.0, r22)], axis=0)
    second = jnp.concatenate([jnp.where(left, r11, u12), jnp.where(left, 0.0, u22)], axis=0)
    return first, second


def factors(flags, own, low):
    shape = (SB, SB)
    eye = rows_of(shape) == lanes(shape)
    first = flags[1] == 1
    own_eye = jnp.where(eye, 1.0, 0.0)
    low_eye = jnp.where(eye & (flags[2] == 1), 1.0, 0.0)
    out = {}
    for which, value in enumerate(assembled(own)):
        out[0, which] = jnp.where(first, own_eye, value)
    for which, value in enumerate(assembled(low)):
        out[1, which] = jnp.where(first, low_eye, value)
    return out


def product(a, b, dims):
    axes = dims[0][0][0], dims[0][1][0]
    left = jnp.concatenate([a[k] for k in (1, 0, 0)], axis=axes[0])
    right = jnp.concatenate([b[k] for k in (0, 1, 0)], axis=axes[1])
    return dot(left, right, dims)


def halves(both):
    return jnp.where(lanes((HALF, SB)) < HALF, both[:HALF, :], both[HALF:, :])


def slabs_of(x):
    return [x[PANEL * t : PANEL * (t + 1), :] for t in range(SLABS)]


def grams(flags, parts_of, at_ref):
    blocks = {}
    for key, start, number in GROUPS:
        lhs = at_ref[start * SB : (start + number) * SB, :]
        pieces = parts_of[key]
        total = dot(jnp.concatenate([lhs] * len(pieces), axis=1), jnp.concatenate(pieces[::-1], axis=1), NT)
        for k in range(number):
            blocks[ORDER[start + k]] = total[k * SB : (k + 1) * SB, :]
    tops = jnp.concatenate([jnp.concatenate([blocks[s, p][:HALF, :] for s in range(2)], axis=0) for p in range(4)], axis=1)
    lows = jnp.concatenate([jnp.concatenate([blocks[s, p][HALF:, :] for s in range(2)], axis=0) for p in range(4)], axis=1)
    tops, lows = split(tops, 2), split(lows, 2)
    both = [jnp.concatenate([a, b], axis=0) for a, b in zip(tops, lows)]
    upper = product(tops, both, NT)
    shape = (HALF, SB)
    live = jnp.where(lanes(shape) < HALF, flags[3], flags[4])
    row = rows_of(shape)
    same = row == (lanes(shape) & (HALF - 1))
    g11 = halves(upper[:, :SB]) + jnp.where(same & (row >= live), 1.0, 0.0)
    g22 = halves(product(lows, lows, NT)) + jnp.where(same & (row + HALF >= live), 1.0, 0.0)
    return g11, halves(upper[:, SB:]), g22


def factorize(flags, parts_of, at_ref, u_ref, w_ref):
    g11, g12, g22 = grams(flags, parts_of, at_ref)
    lane, sub = lanes(), rows_of()
    place = lane & (HALF - 1)
    kept = jnp.where(lane < HALF, flags[5], flags[6])
    scaling = math.sqrt(4 * SB)
    eye = [jnp.where(place == sub + PANEL * t, 1.0, 0.0) for t in range(SLABS)]
    u12, w11 = [], []

    def first(t, head, rest, diag):
        row = sub + PANEL * t
        root = lax.rsqrt(diag)
        at = slice(PANEL * t, PANEL * (t + 1))
        u12.append(rest[0] * root)
        u_ref[at, :] = jnp.where((place >= row) & (row < kept), head * root, 0.0)
        u_ref[slice(at.start + HALF, at.stop + HALF), :] = jnp.where(row < kept, u12[t], 0.0)
        if w_ref is not None:
            w11.append(rest[1] * root)
            w_ref[at, :] = jnp.where(row < kept, w11[t] * scaling, 0.0)

    sweep(slabs_of(g11), [slabs_of(g12)] + ([eye] if w_ref is not None else []), first)
    cross = split(jnp.concatenate(u12, axis=0), 2)
    others = []
    if w_ref is not None:
        below = halves(product(cross, split(jnp.concatenate(w11, axis=0), 2), TN))
        others = [slabs_of(-below), eye]

    def second(t, head, rest, diag):
        row = sub + PANEL * t
        stay = row + HALF < kept
        root = lax.rsqrt(diag)
        u_ref[2 * HALF + PANEL * t : 2 * HALF + PANEL * (t + 1), :] = jnp.where((place >= row) & stay, head * root, 0.0)
        for k, value in enumerate(rest):
            at = HALF * (k + 1) + PANEL * t
            w_ref[at : at + PANEL, :] = jnp.where(stay, value * (root * scaling), 0.0)

    sweep(slabs_of(g22 - halves(product(cross, cross, TN))), others, second)


def round_kernel(at, flags, low_ref, own_ref, at_ref, _, out_ref, state_ref):
    @pl.when(flags[0] == at)
    def _():
        own, low = own_ref[...], low_ref[...]
        state_ref[0], state_ref[1] = own, low
        found = factors(flags, own, low)
        factorize(flags, {k: split(v, 2) for k, v in found.items()}, at_ref, out_ref, None)


def last_kernel(at, flags, low_ref, own_ref, state_ref, at_ref, a_ref, out_ref, w_ref, u_ref):
    here = flags[0] == at
    own = jnp.where(here, own_ref[...], state_ref[0])
    low = jnp.where(here, low_ref[...], state_ref[1])
    found = factors(flags, own, low)
    pair = {k: split(v, 2) for k, v in found.items()}
    factorize(flags, pair, at_ref, u_ref, w_ref)
    met = {}
    for key, start, number in GROUPS:
        for k in range(number):
            met[ORDER[start + k]] = (key, start + k)
    left = lanes((HALF, SB)) < HALF
    w11, w21, w22 = (w_ref[HALF * k : HALF * (k + 1), :] for k in range(3))
    r11, r21, r22 = (pltpu.roll(w, HALF, 1) for w in (w11, w21, w22))
    inverse = (
        jnp.concatenate([jnp.where(left, w11, 0.0), jnp.where(left, w21, r22)], axis=0),
        jnp.concatenate([jnp.where(left, r11, 0.0), jnp.where(left, r21, w22)], axis=0),
    )
    factor = assembled(u_ref[...])
    for s in range(2):
        w_hi, w_lo = split(inverse[s], 2)
        for p in range(4):
            key, start = met[s, p]
            core = a_ref[start * SB : (start + 1) * SB, :]
            turned = dot(core, w_lo, NT) + dot(core, w_hi, NT)
            t_hi, t_lo = split(turned, 2)
            p_hi, p_lo = pair[key]
            block = (dot(p_lo, t_hi, NN) + dot(p_hi, t_lo, NN)) + dot(p_hi, t_hi, NN)
            out_ref[:, s * 16 + p * 4 : s * 16 + p * 4 + 4, :] = block.reshape(32, 4, SB)
        out_ref[:, 32 + 4 * s : 36 + 4 * s, :] = factor[s].reshape(32, 4, SB)


def shards(mps_cores, live_sizes, retained_sizes, pattern):
    n_site = lax.axis_size("site")
    n_row = lax.axis_size("row")
    site_at = lax.axis_index("site")
    row_at = lax.axis_index("row")
    sent = mps_cores.reshape(n_row, 32, SB)
    got = lax.all_to_all(sent, "row", split_axis=0, concat_axis=0, tiled=True)
    got = got.reshape(n_row, 2, 4, 4, SB)
    live, kept = live_sizes[0], retained_sizes[0]
    column = lax.broadcasted_iota(jnp.int32, (2, 4, SB), 2)
    mask = (column < live[:, None, None]) & (pattern[0][:, :, None] != 0)
    cores = jnp.transpose(got, (1, 2, 0, 3, 4)).reshape(2, 4, SB, SB)
    cores = jnp.where(mask[:, :, None, :], cores, jnp.zeros((), cores.dtype))
    stacked = jnp.stack([cores[s, p] for s, p in ORDER])
    a_all = stacked.reshape(8 * SB, SB)
    at_all = jnp.swapaxes(stacked, 1, 2).reshape(8 * SB, SB)
    head = jnp.stack([site_at, (site_at == 0).astype(jnp.int32), (row_at > 0).astype(jnp.int32)])
    flags = jnp.concatenate([head.astype(jnp.int32), live, kept])
    params = pltpu.CompilerParams(vmem_limit_bytes=VMEM_BYTES)
    packet = jax.ShapeDtypeStruct(PACKET, F32)
    own = low = jnp.zeros(PACKET, F32)
    state = jnp.zeros((2,) + PACKET, F32)
    for at in range(n_site - 1):
        factor, state = pl.pallas_call(
            functools.partial(round_kernel, at),
            out_shape=(packet, jax.ShapeDtypeStruct(state.shape, F32)),
            in_specs=[SMEM_SPEC] + [VMEM_SPEC] * 4,
            out_specs=(VMEM_SPEC, VMEM_SPEC),
            input_output_aliases={4: 1},
            compiler_params=params,
            name="round",
        )(flags, low, own, at_all, state)
        here, there = n_row * at, n_row * (at + 1)
        own = lax.ppermute(factor, ("site", "row"), [(here + i, there + i) for i in range(n_row)])
        low = lax.ppermute(factor, ("site", "row"), [(here + i, there + i + 1) for i in range(n_row - 1)])
    out = pl.pallas_call(
        functools.partial(last_kernel, n_site - 1),
        out_shape=jax.ShapeDtypeStruct((32, 40, SB), F32),
        in_specs=[SMEM_SPEC] + [VMEM_SPEC] * 5,
        out_specs=VMEM_SPEC,
        scratch_shapes=[pltpu.VMEM(PACKET, F32), pltpu.VMEM(PACKET, F32)],
        compiler_params=params,
        name="last",
    )(flags, low, own, state, at_all, a_all)
    back = lax.all_to_all(out, "row", split_axis=0, concat_axis=0, tiled=True)
    ortho = back[:, :32].reshape(1, 2 * n_row, 4, 4, SB)
    factor = back[:, 32:].reshape(1, 2 * n_row, 4, SB)
    return (ortho, factor)


def solution(mesh):
    in_specs = (
        P("site", None, None, "row", None),
        P("site", "row"),
        P("site", "row"),
        P("site", "row", None),
    )
    out_specs = (P("site", None, None, "row", None), P("site", None, "row", None))
    return jax.shard_map(shards, mesh=mesh, in_specs=in_specs, out_specs=out_specs, check_vma=False)
```

```python
import functools
import math

import jax
import jax.numpy as jnp
from jax import lax
from jax.experimental import pallas as pl
from jax.experimental.pallas import tpu as pltpu
from jax.sharding import PartitionSpec as P

SB = 128
PANEL = 8
F32 = jnp.float32
BF16 = jnp.bfloat16
NN = (((1,), (0,)), ((), ()))
NT = (((1,), (1,)), ((), ()))
TN = (((0,), (0,)), ((), ()))
VMEM_BYTES = 24 * 1024 * 1024
VMEM_SPEC = pl.BlockSpec(memory_space=pltpu.VMEM)
SMEM_SPEC = pl.BlockSpec(memory_space=pltpu.SMEM)


def dot(a, b, dims):
    return lax.dot_general(a, b, dims, preferred_element_type=F32)


def split(x, parts):
    out = []
    for _ in range(parts):
        piece = x.astype(BF16)
        out.append(piece)
        x = x - piece.astype(F32)
    return out


HALF = SB // 2
SLABS = HALF // PANEL


def lanes(shape=(PANEL, SB)):
    return lax.broadcasted_iota(jnp.int32, shape, 1)


def rows_of(shape=(PANEL, SB)):
    return lax.broadcasted_iota(jnp.int32, shape, 0)


def row_spread(x, i):
    return jnp.broadcast_to(x[i : i + 1, :], (PANEL, SB))


def sweep(main, others, emit):
    lane, sub = lanes(), rows_of()
    high = jnp.where(lane >= HALF, HALF, 0)

    def spread(x, j):
        return jnp.take_along_axis(x, high + j, axis=1, mode="promise_in_bounds")

    tables = [list(main)] + [list(o) for o in others]
    for t in range(SLABS):
        base = PANEL * t
        cols = [spread(tables[0][t], i) for i in range(PANEL)] if t == 0 else ahead
        nxt = t + 1 if t + 1 < SLABS else None
        ahead = [spread(tables[0][nxt], base + PANEL + i) for i in range(PANEL)] if nxt else None
        close = range(t + 1, min(t + 2 + 1, SLABS))
        far = range(t + 2 + 1, SLABS)
        near = {u: [spread(tables[0][u], base + i) for i in range(PANEL)] for u in close}
        fc = {u: [spread(tables[0][u], base + i) for i in range(PANEL)] for u in far}
        diag = None
        ws = [[] for _ in tables]
        ls = {}
        for i in range(PANEL):
            c = cols[i]
            diag = c if i == 0 else jnp.where(sub == i, c, diag)
            inv = row_spread(1.0 / c, i)
            li = jnp.where(sub > i, c, 0.0) * inv
            for m in range(i + 1, PANEL):
                cols[m] = cols[m] - li * row_spread(cols[m], i)
                ls[m, i] = row_spread(li, m)
            for w, table in zip(ws, tables):
                row = row_spread(table[t], i)
                w.append(row * inv)
                if i < PANEL - 1:
                    table[t] = table[t] - li * row
                for u in close:
                    table[u] = table[u] - near[u][i] * w[i]
            for u in close:
                for m in range(i + 1, PANEL):
                    near[u][m] = near[u][m] - near[u][i] * ls[m, i]
            if nxt:
                part = near[nxt][i] * inv
                for m in range(PANEL):
                    ahead[m] = ahead[m] - near[nxt][i] * row_spread(part, m)
        emit(t, tables[0][t], [table[t] for table in tables[1:]], diag)
        if not len(far):
            continue
        for z, table in zip(ws, tables):
            for i in range(PANEL - 2, -1, -1):
                for m in range(PANEL - 1, i, -1):
                    z[i] = z[i] - ls[m, i] * z[m]
            for u in far:
                total = fc[u][0] * z[0]
                for i in range(1, PANEL):
                    total = total + fc[u][i] * z[i]
                table[u] = table[u] - total


ORDER = ((0, 0), (1, 1), (1, 2), (1, 0), (0, 1), (0, 2), (1, 3), (0, 3))
GROUPS = (((0, 0), 0, 3), ((0, 1), 3, 1), ((1, 1), 4, 3), ((1, 0), 7, 1))
PACKET = (3 * HALF, SB)


def assembled(packet):
    left = lanes((HALF, SB)) < HALF
    u11, u12, u22 = (packet[HALF * k : HALF * (k + 1), :] for k in range(3))
    r11, r12, r22 = (pltpu.roll(u, HALF, 1) for u in (u11, u12, u22))
    first = jnp.concatenate([jnp.where(left, u11, r12), jnp.where(left, 0.0, r22)], axis=0)
    second = jnp.concatenate([jnp.where(left, r11, u12), jnp.where(left, 0.0, u22)], axis=0)
    return first, second


def factors(flags, own, low):
    shape = (SB, SB)
    eye = rows_of(shape) == lanes(shape)
    first = flags[1] == 1
    own_eye = jnp.where(eye, 1.0, 0.0)
    low_eye = jnp.where(eye & (flags[2] == 1), 1.0, 0.0)
    out = {}
    for which, value in enumerate(assembled(own)):
        out[0, which] = jnp.where(first, own_eye, value)
    for which, value in enumerate(assembled(low)):
        out[1, which] = jnp.where(first, low_eye, value)
    return out


def product(a, b, dims):
    axes = dims[0][0][0], dims[0][1][0]
    left = jnp.concatenate([a[k] for k in (1, 0, 0)], axis=axes[0])
    right = jnp.concatenate([b[k] for k in (0, 1, 0)], axis=axes[1])
    return dot(left, right, dims)


def halves(both):
    return jnp.where(lanes((HALF, SB)) < HALF, both[:HALF, :], both[HALF:, :])


def slabs_of(x):
    return [x[PANEL * t : PANEL * (t + 1), :] for t in range(SLABS)]


def grams(flags, parts_of, at_ref):
    blocks = {}
    for key, start, number in GROUPS:
        lhs = at_ref[start * SB : (start + number) * SB, :]
        pieces = parts_of[key]
        total = dot(jnp.concatenate([lhs] * len(pieces), axis=1), jnp.concatenate(pieces[::-1], axis=1), NT)
        for k in range(number):
            blocks[ORDER[start + k]] = total[k * SB : (k + 1) * SB, :]
    tops = jnp.concatenate([jnp.concatenate([blocks[s, p][:HALF, :] for s in range(2)], axis=0) for p in range(4)], axis=1)
    lows = jnp.concatenate([jnp.concatenate([blocks[s, p][HALF:, :] for s in range(2)], axis=0) for p in range(4)], axis=1)
    tops, lows = split(tops, 2), split(lows, 2)
    both = [jnp.concatenate([a, b], axis=0) for a, b in zip(tops, lows)]
    upper = product(tops, both, NT)
    shape = (HALF, SB)
    live = jnp.where(lanes(shape) < HALF, flags[3], flags[4])
    row = rows_of(shape)
    same = row == (lanes(shape) & (HALF - 1))
    g11 = halves(upper[:, :SB]) + jnp.where(same & (row >= live), 1.0, 0.0)
    g22 = halves(product(lows, lows, NT)) + jnp.where(same & (row + HALF >= live), 1.0, 0.0)
    return g11, halves(upper[:, SB:]), g22


def factorize(flags, parts_of, at_ref, u_ref, w_ref):
    g11, g12, g22 = grams(flags, parts_of, at_ref)
    lane, sub = lanes(), rows_of()
    place = lane & (HALF - 1)
    kept = jnp.where(lane < HALF, flags[5], flags[6])
    scaling = math.sqrt(4 * SB)
    eye = [jnp.where(place == sub + PANEL * t, 1.0, 0.0) for t in range(SLABS)]
    u12, w11 = [], []

    def first(t, head, rest, diag):
        row = sub + PANEL * t
        root = lax.rsqrt(diag)
        at = slice(PANEL * t, PANEL * (t + 1))
        u12.append(rest[0] * root)
        u_ref[at, :] = jnp.where((place >= row) & (row < kept), head * root, 0.0)
        u_ref[slice(at.start + HALF, at.stop + HALF), :] = jnp.where(row < kept, u12[t], 0.0)
        if w_ref is not None:
            w11.append(rest[1] * root)
            w_ref[at, :] = jnp.where(row < kept, w11[t] * scaling, 0.0)

    sweep(slabs_of(g11), [slabs_of(g12)] + ([eye] if w_ref is not None else []), first)
    cross = split(jnp.concatenate(u12, axis=0), 2)
    others = []
    if w_ref is not None:
        below = halves(product(cross, split(jnp.concatenate(w11, axis=0), 2), TN))
        others = [slabs_of(-below), eye]

    def second(t, head, rest, diag):
        row = sub + PANEL * t
        stay = row + HALF < kept
        root = lax.rsqrt(diag)
        u_ref[2 * HALF + PANEL * t : 2 * HALF + PANEL * (t + 1), :] = jnp.where((place >= row) & stay, head * root, 0.0)
        for k, value in enumerate(rest):
            at = HALF * (k + 1) + PANEL * t
            w_ref[at : at + PANEL, :] = jnp.where(stay, value * (root * scaling), 0.0)

    sweep(slabs_of(g22 - halves(product(cross, cross, TN))), others, second)


def round_kernel(at, flags, own_ref, low_ref, at_ref, _, out_ref, state_ref):
    @pl.when(flags[0] == at)
    def _():
        own, low = own_ref[...], low_ref[...]
        state_ref[0], state_ref[1] = own, low
        found = factors(flags, own, low)
        factorize(flags, {k: split(v, 2) for k, v in found.items()}, at_ref, out_ref, None)


def last_kernel(at, flags, own_ref, low_ref, state_ref, at_ref, a_ref, out_ref, w_ref, u_ref):
    here = flags[0] == at
    own = jnp.where(here, own_ref[...], state_ref[0])
    low = jnp.where(here, low_ref[...], state_ref[1])
    found = factors(flags, own, low)
    pair = {k: split(v, 2) for k, v in found.items()}
    factorize(flags, pair, at_ref, u_ref, w_ref)
    met = {}
    for key, start, number in GROUPS:
        for k in range(number):
            met[ORDER[start + k]] = (key, start + k)
    left = lanes((HALF, SB)) < HALF
    w11, w21, w22 = (w_ref[HALF * k : HALF * (k + 1), :] for k in range(3))
    r11, r21, r22 = (pltpu.roll(w, HALF, 1) for w in (w11, w21, w22))
    inverse = (
        jnp.concatenate([jnp.where(left, w11, 0.0), jnp.where(left, w21, r22)], axis=0),
        jnp.concatenate([jnp.where(left, r11, 0.0), jnp.where(left, r21, w22)], axis=0),
    )
    factor = assembled(u_ref[...])
    for s in range(2):
        w_hi, w_lo = split(inverse[s], 2)
        for p in range(4):
            key, start = met[s, p]
            core = a_ref[start * SB : (start + 1) * SB, :]
            turned = dot(core, w_lo, NT) + dot(core, w_hi, NT)
            t_hi, t_lo = split(turned, 2)
            p_hi, p_lo = pair[key]
            block = (dot(p_lo, t_hi, NN) + dot(p_hi, t_lo, NN)) + dot(p_hi, t_hi, NN)
            out_ref[:, s * 16 + p * 4 : s * 16 + p * 4 + 4, :] = block.reshape(32, 4, SB)
        out_ref[:, 32 + 4 * s : 36 + 4 * s, :] = factor[s].reshape(32, 4, SB)


def shards(mps_cores, live_sizes, retained_sizes, pattern):
    n_site = lax.axis_size("site")
    n_row = lax.axis_size("row")
    site_at = lax.axis_index("site")
    row_at = lax.axis_index("row")
    sent = mps_cores.reshape(n_row, 32, SB)
    got = lax.all_to_all(sent, "row", split_axis=0, concat_axis=0, tiled=True)
    got = got.reshape(n_row, 2, 4, 4, SB)
    live, kept = live_sizes[0], retained_sizes[0]
    column = lax.broadcasted_iota(jnp.int32, (2, 4, SB), 2)
    mask = (column < live[:, None, None]) & (pattern[0][:, :, None] != 0)
    cores = jnp.transpose(got, (1, 2, 0, 3, 4)).reshape(2, 4, SB, SB)
    cores = jnp.where(mask[:, :, None, :], cores, jnp.zeros((), cores.dtype))
    stacked = jnp.stack([cores[s, p] for s, p in ORDER])
    a_all = stacked.reshape(8 * SB, SB)
    at_all = jnp.swapaxes(stacked, 1, 2).reshape(8 * SB, SB)
    head = jnp.stack([site_at, (site_at == 0).astype(jnp.int32), (row_at > 0).astype(jnp.int32)])
    flags = jnp.concatenate([head.astype(jnp.int32), live, kept])
    params = pltpu.CompilerParams(vmem_limit_bytes=VMEM_BYTES)
    packet = jax.ShapeDtypeStruct(PACKET, F32)
    own = low = jnp.zeros(PACKET, F32)
    state = jnp.zeros((2,) + PACKET, F32)
    for at in range(n_site - 1):
        factor, state = pl.pallas_call(
            functools.partial(round_kernel, at),
            out_shape=(packet, jax.ShapeDtypeStruct(state.shape, F32)),
            in_specs=[SMEM_SPEC] + [VMEM_SPEC] * 4,
            out_specs=(VMEM_SPEC, VMEM_SPEC),
            input_output_aliases={4: 1},
            compiler_params=params,
            name="round",
        )(flags, own, low, at_all, state)
        here, there = n_row * at, n_row * (at + 1)
        own = lax.ppermute(factor, ("site", "row"), [(here + i, there + i) for i in range(n_row)])
        low = lax.ppermute(factor, ("site", "row"), [(here + i, there + i + 1) for i in range(n_row - 1)])
    out = pl.pallas_call(
        functools.partial(last_kernel, n_site - 1),
        out_shape=jax.ShapeDtypeStruct((32, 40, SB), F32),
        in_specs=[SMEM_SPEC] + [VMEM_SPEC] * 5,
        out_specs=VMEM_SPEC,
        scratch_shapes=[pltpu.VMEM(PACKET, F32), pltpu.VMEM(PACKET, F32)],
        compiler_params=params,
        name="last",
    )(flags, own, low, state, at_all, a_all)
    back = lax.all_to_all(out, "row", split_axis=0, concat_axis=0, tiled=True)
    ortho = back[:, :32].reshape(1, 2 * n_row, 4, 4, SB)
    factor = back[:, 32:].reshape(1, 2 * n_row, 4, SB)
    return (ortho, factor)


def solution(mesh):
    in_specs = (
        P("site", None, None, "row", None),
        P("site", "row"),
        P("site", "row"),
        P("site", "row", None),
    )
    out_specs = (P("site", None, None, "row", None), P("site", None, "row", None))
    return jax.shard_map(shards, mesh=mesh, in_specs=in_specs, out_specs=out_specs, check_vma=False)
```

```python
import functools
import math

import jax
import jax.numpy as jnp
from jax import lax
from jax.experimental import pallas as pl
from jax.experimental.pallas import tpu as pltpu
from jax.sharding import PartitionSpec as P

SB = 128
PANEL = 8
F32 = jnp.float32
BF16 = jnp.bfloat16
NN = (((1,), (0,)), ((), ()))
NT = (((1,), (1,)), ((), ()))
TN = (((0,), (0,)), ((), ()))
VMEM_BYTES = 24 * 1024 * 1024
VMEM_SPEC = pl.BlockSpec(memory_space=pltpu.VMEM)
SMEM_SPEC = pl.BlockSpec(memory_space=pltpu.SMEM)


def dot(a, b, dims):
    return lax.dot_general(a, b, dims, preferred_element_type=F32)


def split(x, parts):
    out = []
    for _ in range(parts):
        piece = x.astype(BF16)
        out.append(piece)
        x = x - piece.astype(F32)
    return out


HALF = SB // 2
SLABS = HALF // PANEL


def lanes(shape=(PANEL, SB)):
    return lax.broadcasted_iota(jnp.int32, shape, 1)


def rows_of(shape=(PANEL, SB)):
    return lax.broadcasted_iota(jnp.int32, shape, 0)


def row_spread(x, i):
    return jnp.broadcast_to(x[i : i + 1, :], (PANEL, SB))


def sweep(main, others, emit):
    lane, sub = lanes(), rows_of()
    high = jnp.where(lane >= HALF, HALF, 0)

    def spread(x, j):
        return jnp.take_along_axis(x, high + j, axis=1, mode="promise_in_bounds")

    tables = [list(main)] + [list(o) for o in others]
    for t in range(SLABS):
        base = PANEL * t
        cols = [spread(tables[0][t], i) for i in range(PANEL)] if t == 0 else ahead
        nxt = t + 1 if t + 1 < SLABS else None
        ahead = [spread(tables[0][nxt], base + PANEL + i) for i in range(PANEL)] if nxt else None
        close = range(t + 1, min(t + 2 + 1, SLABS))
        far = range(t + 2 + 1, SLABS)
        near = {u: [spread(tables[0][u], base + i) for i in range(PANEL)] for u in close}
        fc = {u: [spread(tables[0][u], base + i) for i in range(PANEL)] for u in far}
        diag = None
        ws = [[] for _ in tables]
        ls = {}
        for i in range(PANEL):
            c = cols[i]
            diag = c if i == 0 else jnp.where(sub == i, c, diag)
            inv = row_spread(1.0 / c, i)
            li = jnp.where(sub > i, c, 0.0) * inv
            for m in range(i + 1, PANEL):
                cols[m] = cols[m] - li * row_spread(cols[m], i)
                ls[m, i] = row_spread(li, m)
            for w, table in zip(ws, tables):
                row = row_spread(table[t], i)
                w.append(row * inv)
                if i < PANEL - 1:
                    table[t] = table[t] - li * row
                for u in close:
                    table[u] = table[u] - near[u][i] * w[i]
            for u in close:
                for m in range(i + 1, PANEL):
                    near[u][m] = near[u][m] - near[u][i] * ls[m, i]
            if nxt:
                part = near[nxt][i] * inv
                for m in range(PANEL):
                    ahead[m] = ahead[m] - near[nxt][i] * row_spread(part, m)
        emit(t, tables[0][t], [table[t] for table in tables[1:]], diag)
        if not len(far):
            continue
        for z, table in zip(ws, tables):
            for i in range(PANEL - 2, -1, -1):
                for m in range(PANEL - 1, i, -1):
                    z[i] = z[i] - ls[m, i] * z[m]
            for u in far:
                total = fc[u][0] * z[0]
                for i in range(1, PANEL):
                    total = total + fc[u][i] * z[i]
                table[u] = table[u] - total


ORDER = ((0, 0), (1, 1), (1, 2), (1, 0), (0, 1), (0, 2), (1, 3), (0, 3))
GROUPS = (((0, 0), 0, 3), ((0, 1), 3, 1), ((1, 1), 4, 3), ((1, 0), 7, 1))
PACKET = (3 * HALF, SB)


def assembled(packet):
    left = lanes((HALF, SB)) < HALF
    u11, u12, u22 = (packet[HALF * k : HALF * (k + 1), :] for k in range(3))
    r11, r12, r22 = (pltpu.roll(u, HALF, 1) for u in (u11, u12, u22))
    first = jnp.concatenate([jnp.where(left, u11, r12), jnp.where(left, 0.0, r22)], axis=0)
    second = jnp.concatenate([jnp.where(left, r11, u12), jnp.where(left, 0.0, u22)], axis=0)
    return first, second


def factors(flags, own, low):
    shape = (SB, SB)
    eye = rows_of(shape) == lanes(shape)
    first = flags[1] == 1
    own_eye = jnp.where(eye, 1.0, 0.0)
    low_eye = jnp.where(eye & (flags[2] == 1), 1.0, 0.0)
    out = {}
    for which, value in enumerate(assembled(own)):
        out[0, which] = jnp.where(first, own_eye, value)
    for which, value in enumerate(assembled(low)):
        out[1, which] = jnp.where(first, low_eye, value)
    return out


def product(a, b, dims):
    axes = dims[0][0][0], dims[0][1][0]
    left = jnp.concatenate([a[k] for k in (1, 0, 0)], axis=axes[0])
    right = jnp.concatenate([b[k] for k in (0, 1, 0)], axis=axes[1])
    return dot(left, right, dims)


def halves(both):
    return jnp.where(lanes((HALF, SB)) < HALF, both[:HALF, :], both[HALF:, :])


def slabs_of(x):
    return [x[PANEL * t : PANEL * (t + 1), :] for t in range(SLABS)]


def grams(flags, parts_of, at_ref):
    blocks = {}
    for key, start, number in GROUPS:
        lhs = at_ref[start * SB : (start + number) * SB, :]
        pieces = parts_of[key]
        total = dot(jnp.concatenate([lhs] * len(pieces), axis=1), jnp.concatenate(pieces[::-1], axis=1), NT)
        for k in range(number):
            blocks[ORDER[start + k]] = total[k * SB : (k + 1) * SB, :]
    tops = jnp.concatenate([jnp.concatenate([blocks[s, p][:HALF, :] for s in range(2)], axis=0) for p in range(4)], axis=1)
    lows = jnp.concatenate([jnp.concatenate([blocks[s, p][HALF:, :] for s in range(2)], axis=0) for p in range(4)], axis=1)
    tops, lows = split(tops, 2), split(lows, 2)
    both = [jnp.concatenate([a, b], axis=0) for a, b in zip(tops, lows)]
    upper = product(tops, both, NT)
    shape = (HALF, SB)
    live = jnp.where(lanes(shape) < HALF, flags[3], flags[4])
    row = rows_of(shape)
    same = row == (lanes(shape) & (HALF - 1))
    g11 = halves(upper[:, :SB]) + jnp.where(same & (row >= live), 1.0, 0.0)
    g22 = halves(product(lows, lows, NT)) + jnp.where(same & (row + HALF >= live), 1.0, 0.0)
    return g11, halves(upper[:, SB:]), g22


def factorize(flags, parts_of, at_ref, u_ref, w_ref):
    g11, g12, g22 = grams(flags, parts_of, at_ref)
    lane, sub = lanes(), rows_of()
    place = lane & (HALF - 1)
    kept = jnp.where(lane < HALF, flags[5], flags[6])
    scaling = math.sqrt(4 * SB)
    eye = [jnp.where(place == sub + PANEL * t, 1.0, 0.0) for t in range(SLABS)]
    u12, w11 = [], []

    def first(t, head, rest, diag):
        row = sub + PANEL * t
        root = lax.rsqrt(diag)
        at = slice(PANEL * t, PANEL * (t + 1))
        u12.append(rest[0] * root)
        u_ref[at, :] = jnp.where((place >= row) & (row < kept), head * root, 0.0)
        u_ref[slice(at.start + HALF, at.stop + HALF), :] = jnp.where(row < kept, u12[t], 0.0)
        if w_ref is not None:
            w11.append(rest[1] * root)
            w_ref[at, :] = jnp.where(row < kept, w11[t] * scaling, 0.0)

    sweep(slabs_of(g11), [slabs_of(g12)] + ([eye] if w_ref is not None else []), first)
    cross = split(jnp.concatenate(u12, axis=0), 2)
    others = []
    if w_ref is not None:
        below = halves(product(cross, split(jnp.concatenate(w11, axis=0), 2), TN))
        others = [slabs_of(-below), eye]

    def second(t, head, rest, diag):
        row = sub + PANEL * t
        stay = row + HALF < kept
        root = lax.rsqrt(diag)
        u_ref[2 * HALF + PANEL * t : 2 * HALF + PANEL * (t + 1), :] = jnp.where((place >= row) & stay, head * root, 0.0)
        for k, value in enumerate(rest):
            at = HALF * (k + 1) + PANEL * t
            w_ref[at : at + PANEL, :] = jnp.where(stay, value * (root * scaling), 0.0)

    sweep(slabs_of(g22 - halves(product(cross, cross, TN))), others, second)


def round_kernel(at, flags, own_ref, low_ref, at_ref, _, out_ref, state_ref):
    @pl.when(flags[0] == at)
    def _():
        own, low = own_ref[...], low_ref[...]
        state_ref[0], state_ref[1] = own, low
        found = factors(flags, own, low)
        factorize(flags, {k: split(v, 2) for k, v in found.items()}, at_ref, out_ref, None)


def last_kernel(at, flags, own_ref, low_ref, state_ref, at_ref, a_ref, out_ref, w_ref, u_ref):
    here = flags[0] == at
    own = jnp.where(here, own_ref[...], state_ref[0])
    low = jnp.where(here, low_ref[...], state_ref[1])
    found = factors(flags, own, low)
    pair = {k: split(v, 2) for k, v in found.items()}
    factorize(flags, pair, at_ref, u_ref, w_ref)
    met = {}
    for key, start, number in GROUPS:
        for k in range(number):
            met[ORDER[start + k]] = (key, start + k)
    left = lanes((HALF, SB)) < HALF
    w11, w21, w22 = (w_ref[HALF * k : HALF * (k + 1), :] for k in range(3))
    r11, r21, r22 = (pltpu.roll(w, HALF, 1) for w in (w11, w21, w22))
    inverse = (
        jnp.concatenate([jnp.where(left, w11, 0.0), jnp.where(left, w21, r22)], axis=0),
        jnp.concatenate([jnp.where(left, r11, 0.0), jnp.where(left, r21, w22)], axis=0),
    )
    factor = assembled(u_ref[...])
    for s in range(2):
        cores = jnp.concatenate([a_ref[met[s, p][1] * SB : (met[s, p][1] + 1) * SB, :] for p in range(4)], axis=0)
        w_hi, w_lo = split(inverse[s], 2)
        turned = dot(jnp.concatenate([cores, cores], axis=1), jnp.concatenate([w_lo, w_hi], axis=1), NT)
        t_hi, t_lo = split(turned, 2)
        for p in range(4):
            at = slice(p * SB, (p + 1) * SB)
            block = product(pair[met[s, p][0]], [t_hi[at, :], t_lo[at, :]], NN)
            out_ref[:, s * 16 + p * 4 : s * 16 + p * 4 + 4, :] = block.reshape(32, 4, SB)
        out_ref[:, 32 + 4 * s : 36 + 4 * s, :] = factor[s].reshape(32, 4, SB)


def shards(mps_cores, live_sizes, retained_sizes, pattern):
    n_site = lax.axis_size("site")
    n_row = lax.axis_size("row")
    site_at = lax.axis_index("site")
    row_at = lax.axis_index("row")
    sent = mps_cores.reshape(n_row, 32, SB)
    got = lax.all_to_all(sent, "row", split_axis=0, concat_axis=0, tiled=True)
    got = got.reshape(n_row, 2, 4, 4, SB)
    live, kept = live_sizes[0], retained_sizes[0]
    column = lax.broadcasted_iota(jnp.int32, (2, 4, SB), 2)
    mask = (column < live[:, None, None]) & (pattern[0][:, :, None] != 0)
    cores = jnp.transpose(got, (1, 2, 0, 3, 4)).reshape(2, 4, SB, SB)
    cores = jnp.where(mask[:, :, None, :], cores, jnp.zeros((), cores.dtype))
    stacked = jnp.stack([cores[s, p] for s, p in ORDER])
    a_all = stacked.reshape(8 * SB, SB)
    at_all = jnp.swapaxes(stacked, 1, 2).reshape(8 * SB, SB)
    head = jnp.stack([site_at, (site_at == 0).astype(jnp.int32), (row_at > 0).astype(jnp.int32)])
    flags = jnp.concatenate([head.astype(jnp.int32), live, kept])
    params = pltpu.CompilerParams(vmem_limit_bytes=VMEM_BYTES)
    packet = jax.ShapeDtypeStruct(PACKET, F32)
    own = low = jnp.zeros(PACKET, F32)
    state = jnp.zeros((2,) + PACKET, F32)
    for at in range(n_site - 1):
        factor, state = pl.pallas_call(
            functools.partial(round_kernel, at),
            out_shape=(packet, jax.ShapeDtypeStruct(state.shape, F32)),
            in_specs=[SMEM_SPEC] + [VMEM_SPEC] * 4,
            out_specs=(VMEM_SPEC, VMEM_SPEC),
            input_output_aliases={4: 1},
            compiler_params=params,
            name="round",
        )(flags, own, low, at_all, state)
        here, there = n_row * at, n_row * (at + 1)
        own = lax.ppermute(factor, ("site", "row"), [(here + i, there + i) for i in range(n_row)])
        low = lax.ppermute(factor, ("site", "row"), [(here + i, there + i + 1) for i in range(n_row - 1)])
    out = pl.pallas_call(
        functools.partial(last_kernel, n_site - 1),
        out_shape=jax.ShapeDtypeStruct((32, 40, SB), F32),
        in_specs=[SMEM_SPEC] + [VMEM_SPEC] * 5,
        out_specs=VMEM_SPEC,
        scratch_shapes=[pltpu.VMEM(PACKET, F32), pltpu.VMEM(PACKET, F32)],
        compiler_params=params,
        name="last",
    )(flags, own, low, state, at_all, a_all)
    back = lax.all_to_all(out, "row", split_axis=0, concat_axis=0, tiled=True)
    ortho = back[:, :32].reshape(1, 2 * n_row, 4, 4, SB)
    factor = back[:, 32:].reshape(1, 2 * n_row, 4, SB)
    return (ortho, factor)


def solution(mesh):
    in_specs = (
        P("site", None, None, "row", None),
        P("site", "row"),
        P("site", "row"),
        P("site", "row", None),
    )
    out_specs = (P("site", None, None, "row", None), P("site", None, "row", None))
    return jax.shard_map(shards, mesh=mesh, in_specs=in_specs, out_specs=out_specs, check_vma=False)
```

```python
import functools
import math

import jax
import jax.numpy as jnp
from jax import lax
from jax.experimental import pallas as pl
from jax.experimental.pallas import tpu as pltpu
from jax.sharding import PartitionSpec as P


SB = 128
PANEL = 8
F32 = jnp.float32
BF16 = jnp.bfloat16
NN = (((1,), (0,)), ((), ()))
NT = (((1,), (1,)), ((), ()))
TN = (((0,), (0,)), ((), ()))
VMEM_BYTES = 24 * 1024 * 1024
TURNS = 380
VMEM_SPEC = pl.BlockSpec(memory_space=pltpu.VMEM)
SMEM_SPEC = pl.BlockSpec(memory_space=pltpu.SMEM)


def dot(a, b, dims):
    return lax.dot_general(a, b, dims, preferred_element_type=F32)


def split(x, parts):
    out = []
    for _ in range(parts):
        piece = x.astype(BF16)
        out.append(piece)
        x = x - piece.astype(F32)
    return out


HALF = SB // 2
SLABS = HALF // PANEL


def lanes(shape=(PANEL, SB)):
    return lax.broadcasted_iota(jnp.int32, shape, 1)


def rows_of(shape=(PANEL, SB)):
    return lax.broadcasted_iota(jnp.int32, shape, 0)


def row_spread(x, i):
    return jnp.broadcast_to(x[i : i + 1, :], (PANEL, SB))


def sweep(main, others, emit):
    lane, sub = lanes(), rows_of()
    high = jnp.where(lane >= HALF, HALF, 0)

    def spread(x, j):
        return jnp.take_along_axis(x, high + j, axis=1, mode="promise_in_bounds")

    tables = [list(main)] + [list(o) for o in others]
    for t in range(SLABS):
        base = PANEL * t
        cols = [spread(tables[0][t], i) for i in range(PANEL)] if t == 0 else ahead
        nxt = t + 1 if t + 1 < SLABS else None
        ahead = [spread(tables[0][nxt], base + PANEL + i) for i in range(PANEL)] if nxt else None
        close = range(t + 1, min(t + 2 + 1, SLABS))
        far = range(t + 2 + 1, SLABS)
        near = {u: [spread(tables[0][u], base + i) for i in range(PANEL)] for u in close}
        fc = {u: [spread(tables[0][u], base + i) for i in range(PANEL)] for u in far}
        diag = None
        ws = [[] for _ in tables]
        ls = {}
        for i in range(PANEL):
            c = cols[i]
            diag = c if i == 0 else jnp.where(sub == i, c, diag)
            inv = row_spread(1.0 / c, i)
            li = jnp.where(sub > i, c, 0.0) * inv
            for m in range(i + 1, PANEL):
                cols[m] = cols[m] - li * row_spread(cols[m], i)
                ls[m, i] = row_spread(li, m)
            for w, table in zip(ws, tables):
                row = row_spread(table[t], i)
                w.append(row * inv)
                if i < PANEL - 1:
                    table[t] = table[t] - li * row
                for u in close:
                    table[u] = table[u] - near[u][i] * w[i]
            for u in close:
                for m in range(i + 1, PANEL):
                    near[u][m] = near[u][m] - near[u][i] * ls[m, i]
            if nxt:
                part = near[nxt][i] * inv
                for m in range(PANEL):
                    ahead[m] = ahead[m] - near[nxt][i] * row_spread(part, m)
        emit(t, tables[0][t], [table[t] for table in tables[1:]], diag)
        if not len(far):
            continue
        for z, table in zip(ws, tables):
            for i in range(PANEL - 2, -1, -1):
                for m in range(PANEL - 1, i, -1):
                    z[i] = z[i] - ls[m, i] * z[m]
            for u in far:
                total = fc[u][0] * z[0]
                for i in range(1, PANEL):
                    total = total + fc[u][i] * z[i]
                table[u] = table[u] - total


ORDER = ((0, 0), (1, 1), (1, 2), (1, 0), (0, 1), (0, 2), (1, 3), (0, 3))
GROUPS = (((0, 0), 0, 3), ((0, 1), 3, 1), ((1, 1), 4, 3), ((1, 0), 7, 1))
PACKET = (3 * HALF, SB)


def assembled(packet):
    left = lanes((HALF, SB)) < HALF
    u11, u12, u22 = (packet[HALF * k : HALF * (k + 1), :] for k in range(3))
    r11, r12, r22 = (pltpu.roll(u, HALF, 1) for u in (u11, u12, u22))
    first = jnp.concatenate([jnp.where(left, u11, r12), jnp.where(left, 0.0, r22)], axis=0)
    second = jnp.concatenate([jnp.where(left, r11, u12), jnp.where(left, 0.0, u22)], axis=0)
    return first, second


def factors(flags, own, low):
    shape = (SB, SB)
    eye = rows_of(shape) == lanes(shape)
    first = flags[1] == 1
    own_eye = jnp.where(eye, 1.0, 0.0)
    low_eye = jnp.where(eye & (flags[2] == 1), 1.0, 0.0)
    out = {}
    for which, value in enumerate(assembled(own)):
        out[0, which] = jnp.where(first, own_eye, value)
    for which, value in enumerate(assembled(low)):
        out[1, which] = jnp.where(first, low_eye, value)
    return out


def product(a, b, dims):
    axes = dims[0][0][0], dims[0][1][0]
    left = jnp.concatenate([a[k] for k in (1, 0, 0)], axis=axes[0])
    right = jnp.concatenate([b[k] for k in (0, 1, 0)], axis=axes[1])
    return dot(left, right, dims)


def halves(both):
    return jnp.where(lanes((HALF, SB)) < HALF, both[:HALF, :], both[HALF:, :])


def slabs_of(x):
    return [x[PANEL * t : PANEL * (t + 1), :] for t in range(SLABS)]


def grams(flags, parts_of, at_ref):
    blocks = {}
    for key, start, number in GROUPS:
        lhs = at_ref[start * SB : (start + number) * SB, :]
        pieces = parts_of[key]
        total = dot(jnp.concatenate([lhs] * len(pieces), axis=1), jnp.concatenate(pieces[::-1], axis=1), NT)
        for k in range(number):
            blocks[ORDER[start + k]] = total[k * SB : (k + 1) * SB, :]
    tops = jnp.concatenate([jnp.concatenate([blocks[s, p][:HALF, :] for s in range(2)], axis=0) for p in range(4)], axis=1)
    lows = jnp.concatenate([jnp.concatenate([blocks[s, p][HALF:, :] for s in range(2)], axis=0) for p in range(4)], axis=1)
    tops, lows = split(tops, 2), split(lows, 2)
    both = [jnp.concatenate([a, b], axis=0) for a, b in zip(tops, lows)]
    upper = product(tops, both, NT)
    shape = (HALF, SB)
    live = jnp.where(lanes(shape) < HALF, flags[3], flags[4])
    row = rows_of(shape)
    same = row == (lanes(shape) & (HALF - 1))
    g11 = halves(upper[:, :SB]) + jnp.where(same & (row >= live), 1.0, 0.0)
    g22 = halves(product(lows, lows, NT)) + jnp.where(same & (row + HALF >= live), 1.0, 0.0)
    return g11, halves(upper[:, SB:]), g22


def factorize(flags, parts_of, at_ref, u_ref, w_ref):
    g11, g12, g22 = grams(flags, parts_of, at_ref)
    lane, sub = lanes(), rows_of()
    place = lane & (HALF - 1)
    kept = jnp.where(lane < HALF, flags[5], flags[6])
    scaling = math.sqrt(4 * SB)
    eye = [jnp.where(place == sub + PANEL * t, 1.0, 0.0) for t in range(SLABS)]
    u12, w11 = [], []

    def first(t, head, rest, diag):
        row = sub + PANEL * t
        root = lax.rsqrt(diag)
        at = slice(PANEL * t, PANEL * (t + 1))
        u12.append(rest[0] * root)
        u_ref[at, :] = jnp.where((place >= row) & (row < kept), head * root, 0.0)
        u_ref[slice(at.start + HALF, at.stop + HALF), :] = jnp.where(row < kept, u12[t], 0.0)
        if w_ref is not None:
            w11.append(rest[1] * root)
            w_ref[at, :] = jnp.where(row < kept, w11[t] * scaling, 0.0)

    sweep(slabs_of(g11), [slabs_of(g12)] + ([eye] if w_ref is not None else []), first)
    cross = split(jnp.concatenate(u12, axis=0), 2)
    others = []
    if w_ref is not None:
        below = halves(product(cross, split(jnp.concatenate(w11, axis=0), 2), TN))
        others = [slabs_of(-below), eye]

    def second(t, head, rest, diag):
        row = sub + PANEL * t
        stay = row + HALF < kept
        root = lax.rsqrt(diag)
        u_ref[2 * HALF + PANEL * t : 2 * HALF + PANEL * (t + 1), :] = jnp.where((place >= row) & stay, head * root, 0.0)
        for k, value in enumerate(rest):
            at = HALF * (k + 1) + PANEL * t
            w_ref[at : at + PANEL, :] = jnp.where(stay, value * (root * scaling), 0.0)

    sweep(slabs_of(g22 - halves(product(cross, cross, TN))), others, second)


def round_kernel(at, flags, own_ref, low_ref, at_ref, _, out_ref, state_ref):
    @pl.when(flags[0] == at)
    def _():
        own, low = own_ref[...], low_ref[...]
        state_ref[0], state_ref[1] = own, low
        found = factors(flags, own, low)
        factorize(flags, {k: split(v, 2) for k, v in found.items()}, at_ref, out_ref, None)


def last_kernel(at, flags, own_ref, low_ref, state_ref, at_ref, a_ref, out_ref, w_ref, u_ref):
    here = flags[0] == at
    own = jnp.where(here, own_ref[...], state_ref[0])
    low = jnp.where(here, low_ref[...], state_ref[1])
    found = factors(flags, own, low)
    pair = {k: split(v, 2) for k, v in found.items()}
    factorize(flags, pair, at_ref, u_ref, w_ref)
    met = {}
    for key, start, number in GROUPS:
        for k in range(number):
            met[ORDER[start + k]] = (key, start + k)
    left = lanes((HALF, SB)) < HALF
    w11, w21, w22 = (w_ref[HALF * k : HALF * (k + 1), :] for k in range(3))
    r11, r21, r22 = (pltpu.roll(w, HALF, 1) for w in (w11, w21, w22))
    inverse = (
        jnp.concatenate([jnp.where(left, w11, 0.0), jnp.where(left, w21, r22)], axis=0),
        jnp.concatenate([jnp.where(left, r11, 0.0), jnp.where(left, r21, w22)], axis=0),
    )
    factor = assembled(u_ref[...])
    for s in range(2):
        cores = jnp.concatenate([a_ref[met[s, p][1] * SB : (met[s, p][1] + 1) * SB, :] for p in range(4)], axis=0)
        w_hi, w_lo = split(inverse[s], 2)
        turned = dot(jnp.concatenate([cores, cores], axis=1), jnp.concatenate([w_lo, w_hi], axis=1), NT)
        t_hi, t_lo = split(turned, 2)
        for p in range(4):
            at = slice(p * SB, (p + 1) * SB)
            block = product(pair[met[s, p][0]], [t_hi[at, :], t_lo[at, :]], NN)
            out_ref[:, s * 16 + p * 4 : s * 16 + p * 4 + 4, :] = block.reshape(32, 4, SB)
        out_ref[:, 32 + 4 * s : 36 + 4 * s, :] = factor[s].reshape(32, 4, SB)


def hold_kernel(odd_ref, out_ref):
    def turn(_, value):
        return lax.rem(value * 5 + 3, 8191)

    last = lax.fori_loop(0, odd_ref[0] * TURNS, turn, odd_ref[0])
    out_ref[0] = jnp.where(last < 0, 1, 0)


def shards(mps_cores, live_sizes, retained_sizes, pattern):
    n_site = lax.axis_size("site")
    n_row = lax.axis_size("row")
    site_at = lax.axis_index("site")
    row_at = lax.axis_index("row")
    sent = mps_cores.reshape(n_row, 32, SB)
    held = pl.pallas_call(
        hold_kernel,
        out_shape=jax.ShapeDtypeStruct((1,), jnp.int32),
        in_specs=[SMEM_SPEC],
        out_specs=SMEM_SPEC,
        name="hold",
    )((site_at % 2).astype(jnp.int32).reshape(1))
    got = lax.all_to_all(sent, "row", split_axis=0, concat_axis=0, tiled=True)
    got = got.reshape(n_row, 2, 4, 4, SB)
    live, kept = live_sizes[0], retained_sizes[0]
    column = lax.broadcasted_iota(jnp.int32, (2, 4, SB), 2)
    mask = (column < live[:, None, None]) & (pattern[0][:, :, None] != 0)
    cores = jnp.transpose(got, (1, 2, 0, 3, 4)).reshape(2, 4, SB, SB)
    cores = jnp.where(mask[:, :, None, :], cores, jnp.zeros((), cores.dtype))
    stacked = jnp.stack([cores[s, p] for s, p in ORDER])
    a_all = stacked.reshape(8 * SB, SB)
    at_all = jnp.swapaxes(stacked, 1, 2).reshape(8 * SB, SB)
    head = jnp.stack([site_at + held[0], (site_at == 0).astype(jnp.int32), (row_at > 0).astype(jnp.int32)])
    flags = jnp.concatenate([head.astype(jnp.int32), live, kept])
    params = pltpu.CompilerParams(vmem_limit_bytes=VMEM_BYTES)
    packet = jax.ShapeDtypeStruct(PACKET, F32)
    own = low = jnp.zeros(PACKET, F32)
    state = jnp.zeros((2,) + PACKET, F32)
    for at in range(n_site - 1):
        factor, state = pl.pallas_call(
            functools.partial(round_kernel, at),
            out_shape=(packet, jax.ShapeDtypeStruct(state.shape, F32)),
            in_specs=[SMEM_SPEC] + [VMEM_SPEC] * 4,
            out_specs=(VMEM_SPEC, VMEM_SPEC),
            input_output_aliases={4: 1},
            compiler_params=params,
            name="round",
        )(flags, own, low, at_all, state)
        here, there = n_row * at, n_row * (at + 1)
        own = lax.ppermute(factor, ("site", "row"), [(here + i, there + i) for i in range(n_row)])
        low = lax.ppermute(factor, ("site", "row"), [(here + i, there + i + 1) for i in range(n_row - 1)])
    out = pl.pallas_call(
        functools.partial(last_kernel, n_site - 1),
        out_shape=jax.ShapeDtypeStruct((32, 40, SB), F32),
        in_specs=[SMEM_SPEC] + [VMEM_SPEC] * 5,
        out_specs=VMEM_SPEC,
        scratch_shapes=[pltpu.VMEM(PACKET, F32), pltpu.VMEM(PACKET, F32)],
        compiler_params=params,
        name="last",
    )(flags, own, low, state, at_all, a_all)
    back = lax.all_to_all(out, "row", split_axis=0, concat_axis=0, tiled=True)
    ortho = back[:, :32].reshape(1, 2 * n_row, 4, 4, SB)
    factor = back[:, 32:].reshape(1, 2 * n_row, 4, SB)
    return (ortho, factor)


def solution(mesh):
    in_specs = (
        P("site", None, None, "row", None),
        P("site", "row"),
        P("site", "row"),
        P("site", "row", None),
    )
    out_specs = (P("site", None, None, "row", None), P("site", None, "row", None))
    return jax.shard_map(shards, mesh=mesh, in_specs=in_specs, out_specs=out_specs, check_vma=False)
```
